32 devices in a mesh: fsdp: 16 (over z, x, core), tensor: 2 (over y).
Axes of the slice: x: 2, y: 2, z: 4, core: 2. Of those that a mesh axis runs over, the one named last changes fastest.
Arguments:
- tokens: bfloat16 [8192, 1024], P(('fsdp', 'tensor')), may hold values from -6 to 6
- segments: int32 [16, 512], P('fsdp'), may hold values from 0 to 3, never falling along the last dimension, each value on 1 to 256 neighbouring positions
- norm_gains: float32 [2, 1024], P(None, ('fsdp', 'tensor')), may hold values from 0.5 to 1.5
- row_biases: float32 [4, 1024], P(None, ('fsdp', 'tensor')), may hold values from -3 to 3
- attention_in: bfloat16 [1024, 3, 1024], P('fsdp', None, 'tensor'), may hold values from -0.1875 to 0.1875
- query_bias: bfloat16 [16, 64], P('tensor', 'fsdp'), may hold values from -3 to 3
- value_bias: bfloat16 [16, 64], P('tensor', 'fsdp'), may hold values from -1.1953125 to 1.1953125
- attention_out: bfloat16 [1024, 1024], P('tensor', 'fsdp'), may hold values from -0.75 to 0.75
- hidden_in: bfloat16 [1024, 4096], P('fsdp', 'tensor'), may hold values from -0.1875 to 0.1875
- hidden_bias: bfloat16 [16, 256], P('tensor', 'fsdp'), may hold values from -3 to 3
- hidden_out: bfloat16 [4096, 1024], P('tensor', 'fsdp'), may hold values from -0.09375 to 0.09375
- output_grad: bfloat16 [8192, 1024], P(('fsdp', 'tensor')), may hold values from -6 to 6
Outputs:
- output: bfloat16 [8192, 1024], P(('fsdp', 'tensor'))
- tokens_grad: bfloat16 [8192, 1024], P(('fsdp', 'tensor'))
- attention_in_grad: float32 [1024, 3, 1024], P('fsdp', None, 'tensor')
- attention_out_grad: float32 [1024, 1024], P('tensor', 'fsdp')
- hidden_in_grad: float32 [1024, 4096], P('fsdp', 'tensor')
- hidden_out_grad: float32 [4096, 1024], P('tensor', 'fsdp')
- query_bias_grad: float32 [16, 64], P('tensor', 'fsdp')
- value_bias_grad: float32 [16, 64], P('tensor', 'fsdp')
- hidden_bias_grad: float32 [16, 256], P('tensor', 'fsdp')
- norm_gains_grad: float32 [2, 1024], P(None, ('fsdp', 'tensor'))
- row_biases_grad: float32 [4, 1024], P(None, ('fsdp', 'tensor'))
The draws below stay inside these ranges and needn't reach their ends.
Inputs may be any that keep to these rules, and one draw needn't show every extreme that they name: `segments`: along each sequence segment numbers never fall; each sequence holds documents of 1 to 256 tokens, one of exactly 256.
All inputs are finite; a program needn't handle non-finite values.
Results may differ from the reference program's by a relative error of at most 0.017.
Values may be sent and summed in bfloat16 or wider, within the bound.
No kernel may reach another device: no remote copies, remote signals or barrier semaphores. Data moves between devices by JAX's collectives and lax.ppermute only.
A program may use at most 128 MiB of HBM per device.

```python
import math
import jax
import jax.numpy as jnp
import numpy as np
from jax import lax

D = 1024
HEADS = 16
HD = 64
FF = 4096
SEQ_LEN = 512
SEQS = 16
TOKENS = 8192
N_TENSOR = 2


def spiked(entries, stream_key, source, target, parts, factor):
    def block_of(position):
        return (jnp.arange(entries.shape[position]) // (entries.shape[position] // parts)).reshape((-1,) + (1,) * (entries.ndim - 1 - position))

    first = jax.random.permutation(stream_key, parts)[block_of(target)]
    far = (block_of(target) + parts // 2) % parts
    return jnp.where((block_of(source) == first) | (block_of(source) == far), factor * entries, entries)


def block_scale(own_key, extent, split, smallest, high):
    level = 1.0
    for dim, blocks in split:
        steps = jax.random.uniform(jax.random.fold_in(jax.random.fold_in(own_key, 6), dim), (blocks,), jnp.float32, smallest / len(split), high / len(split))
        level = level * jnp.repeat(jnp.exp(steps), extent[dim] // blocks).reshape((-1,) + (1,) * (len(extent) - 1 - dim))
    return level


def split_up(number_of, total, reach, slope):
    loads = [(1 << 20) // math.isqrt(standing ** slope) + 1 for standing in range(2, number_of + 1)]
    spare, holding = total - reach - (number_of - 1), [1] * (number_of - 1)
    while spare > 0:
        movable = [i for i in range(number_of - 1) if holding[i] < reach]
        whole, left = sum([loads[i] for i in movable]), spare
        for i in movable:
            extra = min(reach - holding[i], max(1, left * loads[i] // whole), spare)
            holding[i] = holding[i] + extra
            spare = spare - extra
    return np.array([reach] + holding)


def ragged(key, count, total, most, slope):
    if count == 2:
        one = jax.random.randint(key, (), max(1, total - most), min(most, total - 1) + 1)
        return jnp.stack([one, total - one])
    lengths = jnp.asarray(split_up(count, total, most, slope), jnp.int32)
    twos = (count - 1) // 2
    donor, taker = lengths[1:1 + 2 * twos:2], lengths[2:2 + 2 * twos:2]
    room = jnp.minimum(donor - 1, most - taker)
    shifted = jax.random.randint(jax.random.fold_in(key, 1), (twos,), 0, 1 << 20) % (room + 1)
    lengths = lengths.at[1:1 + 2 * twos:2].set(donor - shifted).at[2:2 + 2 * twos:2].set(taker + shifted)
    return lengths[jax.random.permutation(jax.random.fold_in(key, 2), count)]


def gaussian(stream_key, shape, width, bound, split=(), dtype=jnp.bfloat16):
    values = jax.random.normal(stream_key, shape, jnp.float32) * width
    if len(split) > 0:
        values = block_scale(stream_key, shape, split, -0.22, 0.18) * values
    return jnp.clip(values, min=-bound, max=bound).astype(dtype)


def gaussian_with(own_key, shape, scale, bound, cuts, heavy, kind=jnp.bfloat16):
    array = scale * jax.random.normal(own_key, shape, jnp.float32)
    if cuts:
        array = array * block_scale(own_key, shape, cuts, -0.22, 0.18)
    return jnp.clip(spiked(array, jax.random.fold_in(own_key, 3), *heavy), -bound, bound).astype(kind)


def setup_inputs(seed: int = 0) -> dict:
    keys = jax.random.split(jax.random.key(seed), 13)
    tokens = gaussian_with(keys[0], (TOKENS, D), 1.0, 6.0, ((0, 32),), (0, 1, 32, 2.75))
    segments = jax.vmap(lambda own: jnp.searchsorted(jnp.cumsum(ragged(own, 4, SEQ_LEN, SEQ_LEN // 2, 0)), jnp.arange(SEQ_LEN), side="right"))(jax.random.split(keys[1], SEQS)).reshape((SEQS, SEQ_LEN)).astype(jnp.int32)
    norm_gains = jnp.clip(1.0 + 0.1 * jax.random.normal(keys[2], (2, D), jnp.float32), 0.5, 1.5)
    row_biases = gaussian(keys[3], (4, D), 0.5, 3.0, ((1, 32),), jnp.float32)
    attention_in = gaussian(keys[4], (D, 3, D), D ** -0.5, 0.1875, ((0, 16), (2, 2)))
    query_bias = gaussian(keys[5], (HEADS, HD), 0.5, 3.0, ((0, 2), (1, 16)))
    value_bias = gaussian(keys[6], (HEADS, HD), 0.2, 1.1953125, ((0, 2), (1, 16)))
    attention_out = gaussian(keys[7], (D, D), (D // 16) ** -0.5, 0.75, ((0, 2), (1, 16)))
    hidden_in = gaussian(keys[8], (D, FF), D ** -0.5, 0.1875, ((0, 16), (1, 2)))
    hidden_bias = gaussian(keys[9], (HEADS, FF // HEADS), 0.5, 3.0, ((0, 2), (1, 16)))
    hidden_out = gaussian(keys[10], (FF, D), FF ** -0.5, 0.09375, ((0, 2), (1, 16)))
    output_grad = gaussian_with(keys[11], (TOKENS, D), 1.0, 6.0, ((0, 32),), (0, 1, 32, 2.75))
    return {"tokens": tokens, "segments": segments, "norm_gains": norm_gains, "row_biases": row_biases, "attention_in": attention_in, "query_bias": query_bias, "value_bias": value_bias, "attention_out": attention_out, "hidden_in": hidden_in, "hidden_bias": hidden_bias, "hidden_out": hidden_out, "output_grad": output_grad}


EPS = 1e-05
GELU_C = math.sqrt(2.0 / math.pi)
GELU_A = 0.044715
MASKED = -1e+30

def gelu_value(pre_act):
    return 0.5 * pre_act * (1.0 + jnp.tanh(GELU_C * (pre_act + GELU_A * pre_act * pre_act * pre_act)))

def gelu_slope(pre_act):
    tanh_part = jnp.tanh(GELU_C * (pre_act + GELU_A * pre_act * pre_act * pre_act))
    return 0.5 * (1.0 + tanh_part) + 0.5 * pre_act * (1.0 - tanh_part * tanh_part) * GELU_C * (1.0 + 3.0 * GELU_A * pre_act * pre_act)

def normalize(row_data, gain_row, shift_row):
    row_mean = lax.optimization_barrier(jnp.mean(row_data, axis=-1, keepdims=True))
    centered = row_data - row_mean
    variance = lax.optimization_barrier(jnp.mean(centered * centered, axis=-1, keepdims=True))
    inverse = lax.rsqrt(variance + EPS)
    normed = centered * inverse
    return (normed * gain_row + shift_row, normed, inverse)

def normalize_back(grad_rows, normed, inverse, gain_row):
    scaled = grad_rows * gain_row
    return inverse * (scaled - lax.optimization_barrier(jnp.mean(scaled, axis=-1, keepdims=True)) - normed * lax.optimization_barrier(jnp.mean(scaled * normed, axis=-1, keepdims=True)))

def grouped_product(left_side, right_side):
    row_count = left_side.shape[0]
    inner_size = left_side.shape[1] // N_TENSOR
    left_groups = left_side.astype(jnp.float32).reshape(row_count, N_TENSOR, inner_size)
    right_groups = right_side.astype(jnp.float32).reshape(N_TENSOR, inner_size, right_side.shape[1])
    partial_sums = jnp.einsum('tgk,gkd->tgd', left_groups, right_groups)
    rounded = lax.optimization_barrier(partial_sums.astype(jnp.bfloat16))
    return lax.optimization_barrier(jnp.sum(rounded.astype(jnp.float32), axis=1))

def allowed_pairs(segment_row):
    places = jnp.arange(segment_row.shape[0])
    causal = places[:, None] >= places[None, :]
    return causal & (segment_row[:, None] == segment_row[None, :])

def head_scores(query_h, key_h, allowed, score_scale):
    scores = jnp.einsum('qhe,khe->hqk', query_h.astype(jnp.float32), key_h.astype(jnp.float32)) * score_scale
    return jnp.where(allowed, scores, MASKED)

def reference(tokens, segments, norm_gains, row_biases, attention_in, query_bias, value_bias, attention_out, hidden_in, hidden_bias, hidden_out, output_grad):
    seq_count = segments.shape[0]
    seq_len = segments.shape[1]
    model_width = tokens.shape[1]
    head_count = query_bias.shape[0]
    head_size = query_bias.shape[1]
    group_width = model_width // N_TENSOR
    score_scale = 1.0 / math.sqrt(head_size)
    in_flat = attention_in.reshape(model_width, 3 * model_width)
    in_grouped = attention_in.reshape(model_width, 3, N_TENSOR, group_width).transpose(2, 1, 3, 0).reshape(3 * model_width, model_width)
    query_add = query_bias.astype(jnp.float32).reshape(model_width)
    value_add = value_bias.astype(jnp.float32).reshape(model_width)
    hidden_add = hidden_bias.astype(jnp.float32).reshape(-1)
    head_shape = (seq_len, head_count, head_size)

    def one_sequence(totals, inputs):
        tok_seq, grad_seq, seg_seq = inputs
        allowed = allowed_pairs(seg_seq)[None]
        tok_rows = tok_seq.astype(jnp.float32)
        norm_one, normed_one, inverse_one = normalize(tok_rows, norm_gains[0], row_biases[0])
        in_one = norm_one.astype(jnp.bfloat16)
        projected = jnp.dot(in_one, in_flat, preferred_element_type=jnp.float32).reshape(seq_len, 3, model_width)
        query_rows = (projected[:, 0] + query_add).astype(jnp.bfloat16).reshape(head_shape)
        key_rows = projected[:, 1].astype(jnp.bfloat16).reshape(head_shape)
        value_rows = (projected[:, 2] + value_add).astype(jnp.bfloat16).reshape(head_shape)
        scores = head_scores(query_rows, key_rows, allowed, score_scale)
        row_top = lax.optimization_barrier(jnp.max(scores, axis=-1, keepdims=True))
        exp_terms = jnp.exp(scores - row_top)
        exp_total = lax.optimization_barrier(jnp.sum(exp_terms, axis=-1, keepdims=True))
        log_total = row_top + jnp.log(exp_total)
        probs_b = (exp_terms / exp_total).astype(jnp.bfloat16)
        mixed = jnp.einsum('hqk,khe->qhe', probs_b.astype(jnp.float32), value_rows.astype(jnp.float32))
        mixed_rows = mixed.reshape(seq_len, model_width).astype(jnp.bfloat16)
        attn_rows = grouped_product(mixed_rows, attention_out)
        resid_rows = tok_rows + attn_rows + row_biases[1]
        norm_two, normed_two, inverse_two = normalize(resid_rows, norm_gains[1], row_biases[2])
        in_two = norm_two.astype(jnp.bfloat16)
        pre_act = jnp.dot(in_two, hidden_in, preferred_element_type=jnp.float32) + hidden_add
        act_rows = gelu_value(pre_act).astype(jnp.bfloat16)
        mlp_rows = grouped_product(act_rows, hidden_out)
        result = (resid_rows + mlp_rows + row_biases[3]).astype(jnp.bfloat16)
        grad_rows = grad_seq.astype(jnp.float32)
        g_down = jnp.dot(act_rows.T, grad_seq, preferred_element_type=jnp.float32)
        g_act = jnp.dot(grad_seq, hidden_out.T, preferred_element_type=jnp.float32)
        g_pre = g_act * gelu_slope(pre_act)
        g_hidden_add = lax.optimization_barrier(jnp.sum(g_pre, axis=0))
        g_pre_b = g_pre.astype(jnp.bfloat16)
        g_up = jnp.dot(in_two.T, g_pre_b, preferred_element_type=jnp.float32)
        g_norm_two = grouped_product(g_pre_b, hidden_in.T)
        g_resid = grad_rows + normalize_back(g_norm_two, normed_two, inverse_two, norm_gains[1])
        g_resid_b = g_resid.astype(jnp.bfloat16)
        g_out = jnp.dot(mixed_rows.T, g_resid_b, preferred_element_type=jnp.float32)
        g_mixed = jnp.dot(g_resid_b, attention_out.T, preferred_element_type=jnp.float32).astype(jnp.bfloat16)
        g_mixed_h = g_mixed.reshape(head_shape).astype(jnp.float32)
        scores_again = head_scores(query_rows, key_rows, allowed, score_scale)
        probs = jnp.exp(scores_again - log_total)
        probs_again = probs.astype(jnp.bfloat16).astype(jnp.float32)
        g_values = jnp.einsum('hqk,qhe->khe', probs_again, g_mixed_h)
        g_probs = jnp.einsum('qhe,khe->hqk', g_mixed_h, value_rows.astype(jnp.float32))
        inner_sum = lax.optimization_barrier(jnp.sum(probs * g_probs, axis=-1, keepdims=True))
        g_scores = (probs * (g_probs - inner_sum) * score_scale).astype(jnp.bfloat16).astype(jnp.float32)
        g_query = jnp.einsum('hqk,khe->qhe', g_scores, key_rows.astype(jnp.float32)).reshape(seq_len, model_width)
        g_keys = jnp.einsum('hqk,qhe->khe', g_scores, query_rows.astype(jnp.float32)).reshape(seq_len, model_width)
        g_values = g_values.reshape(seq_len, model_width)
        g_query_add = lax.optimization_barrier(jnp.sum(g_query, axis=0))
        g_value_add = lax.optimization_barrier(jnp.sum(g_values, axis=0))
        g_proj = jnp.stack([g_query, g_keys, g_values], axis=1).astype(jnp.bfloat16)
        g_in = jnp.dot(in_one.T, g_proj.reshape(seq_len, 3 * model_width), preferred_element_type=jnp.float32)
        g_proj_grouped = g_proj.reshape(seq_len, 3, N_TENSOR, group_width).transpose(0, 2, 1, 3).reshape(seq_len, 3 * model_width)
        g_norm_one = grouped_product(g_proj_grouped, in_grouped)
        tokens_grad = (g_resid + normalize_back(g_norm_one, normed_one, inverse_one, norm_gains[0])).astype(jnp.bfloat16)
        gain_terms = jnp.stack([lax.optimization_barrier(jnp.sum(g_norm_one * normed_one, axis=0)), lax.optimization_barrier(jnp.sum(g_norm_two * normed_two, axis=0))])
        bias_terms = jnp.stack([lax.optimization_barrier(jnp.sum(g_norm_one, axis=0)), lax.optimization_barrier(jnp.sum(g_resid, axis=0)), lax.optimization_barrier(jnp.sum(g_norm_two, axis=0)), lax.optimization_barrier(jnp.sum(grad_rows, axis=0))])
        terms = (g_in, g_out, g_up, g_down, g_query_add, g_value_add, g_hidden_add, gain_terms, bias_terms)
        new_totals = jax.tree.map(lambda old_sum, new_term: old_sum + new_term, totals, terms)
        return (new_totals, (result, tokens_grad))
    start = (jnp.zeros((model_width, 3 * model_width), jnp.float32), jnp.zeros((model_width, model_width), jnp.float32), jnp.zeros(hidden_in.shape, jnp.float32), jnp.zeros(hidden_out.shape, jnp.float32), jnp.zeros((model_width,), jnp.float32), jnp.zeros((model_width,), jnp.float32), jnp.zeros((hidden_in.shape[1],), jnp.float32), jnp.zeros((2, model_width), jnp.float32), jnp.zeros((4, model_width), jnp.float32))
    sequences = (tokens.reshape(seq_count, seq_len, model_width), output_grad.reshape(seq_count, seq_len, model_width), segments)
    totals, stacked = lax.scan(one_sequence, start, sequences)
    return (stacked[0].reshape(-1, model_width), stacked[1].reshape(-1, model_width), totals[0].reshape(model_width, 3, model_width), totals[1], totals[2], totals[3], totals[4].reshape(head_count, head_size), totals[5].reshape(head_count, head_size), totals[6].reshape(hidden_bias.shape), totals[7], totals[8])
```

```python
import math

import jax
import jax.numpy as jnp
from jax import lax
from jax.sharding import PartitionSpec as P

HD = 64
EPS = 1e-05
GELU_C = math.sqrt(2.0 / math.pi)
GELU_A = 0.044715
MASKED = -1e30
BF16 = jnp.bfloat16
F32 = jnp.float32


def gelu_parts(pre_act):
    square = pre_act * pre_act
    tanh_part = jnp.tanh(GELU_C * pre_act * (1.0 + GELU_A * square))
    half = 0.5 * (1.0 + tanh_part)
    slope = half + 0.5 * pre_act * (1.0 - tanh_part * tanh_part) * GELU_C * (
        1.0 + 3.0 * GELU_A * square
    )
    return pre_act * half, slope


def normalize(row_data):
    row_mean = jnp.mean(row_data, axis=-1, keepdims=True)
    centered = row_data - row_mean
    variance = jnp.mean(centered * centered, axis=-1, keepdims=True)
    inverse = lax.rsqrt(variance + EPS)
    return centered * inverse, inverse


def normalize_back(grad_rows, normed, inverse, gain_row):
    scaled = grad_rows * gain_row
    return inverse * (
        scaled
        - jnp.mean(scaled, axis=-1, keepdims=True)
        - normed * jnp.mean(scaled * normed, axis=-1, keepdims=True)
    )


def pair_mask(segments):
    places = jnp.arange(segments.shape[1])
    causal = places[:, None] >= places[None, :]
    same_doc = segments[:, :, None] == segments[:, None, :]
    return (causal[None] & same_doc)[:, None]


def head_scores(query_rows, key_rows, allowed, score_scale):
    scores = (
        jnp.einsum("sqhe,skhe->shqk", query_rows, key_rows, preferred_element_type=F32)
        * score_scale
    )
    return jnp.where(allowed, scores, MASKED)


def attend(query_rows, key_rows, value_rows, allowed, score_scale):
    scores = head_scores(query_rows, key_rows, allowed, score_scale)
    row_top = jnp.max(scores, axis=-1, keepdims=True)
    exp_terms = jnp.exp(scores - row_top)
    exp_total = jnp.sum(exp_terms, axis=-1, keepdims=True)
    log_total = row_top + jnp.log(exp_total)
    probs_b = (exp_terms / exp_total).astype(BF16)
    mixed = jnp.einsum("shqk,skhe->sqhe", probs_b, value_rows, preferred_element_type=F32)
    return mixed, log_total


def attend_back(query_rows, key_rows, value_rows, allowed, score_scale, log_total, g_mixed):
    scores_again = head_scores(query_rows, key_rows, allowed, score_scale)
    probs = jnp.exp(scores_again - log_total)
    g_values = jnp.einsum(
        "shqk,sqhe->skhe", probs.astype(BF16), g_mixed, preferred_element_type=F32
    )
    g_probs = jnp.einsum("sqhe,skhe->shqk", g_mixed, value_rows, preferred_element_type=F32)
    inner_sum = jnp.sum(probs * g_probs, axis=-1, keepdims=True)
    g_scores = (probs * (g_probs - inner_sum) * score_scale).astype(BF16)
    g_query = jnp.einsum("shqk,skhe->sqhe", g_scores, key_rows, preferred_element_type=F32)
    g_keys = jnp.einsum("shqk,sqhe->skhe", g_scores, query_rows, preferred_element_type=F32)
    return g_query, g_keys, g_values


def dot(left, right, dims):
    return lax.dot_general(left, right, (dims, ((), ())), preferred_element_type=F32)


class Ring:
    def __init__(self, n_fsdp):
        self.size = n_fsdp
        self.cores = 2
        self.second = n_fsdp // 8
        self.first = n_fsdp // (self.second * self.cores)

    def split(self, index):
        return (
            index // (self.second * self.cores),
            (index // self.cores) % self.second,
            index % self.cores,
        )

    def hop(self, value, first=0, second=0, core=0):
        pairs = []
        for source in range(self.size):
            a, b, c = self.split(source)
            a, b, c = (a + first) % self.first, (b + second) % self.second, (c + core) % self.cores
            pairs.append((source, (a * self.second + b) * self.cores + c))
        return lax.ppermute(value, "fsdp", pairs)

    def local_block(self, block):
        a, b, c = self.split(lax.axis_index("fsdp"))
        ga, gb, gc = self.split(block)
        r = (a - ga + self.first) % self.first
        xx = (b - gb + self.second) % self.second
        cc = (c - gc + self.cores) % self.cores
        return (cc * self.second + xx) * self.first + r

    def gather(self, block):
        current = [block]
        for _ in range(self.first - 1):
            current.append(self.hop(current[-1], first=1))
        own = list(current)
        for _ in range(self.second - 1):
            current = [self.hop(piece, second=1) for piece in current]
            own += current
        own = jnp.concatenate(own, axis=0)
        return jnp.concatenate([own, self.hop(own, core=1)], axis=0)

    def gather_small(self, block):
        own = [block] + [self.hop(block, first=r) for r in range(1, self.first)]
        current = own = jnp.concatenate(own, axis=0)
        for _ in range(self.second - 1):
            current = self.hop(current, second=1)
            own = jnp.concatenate([own, current], axis=0)
        return jnp.concatenate([own, self.hop(own, core=1)], axis=0)

    def scatter(self, blocks, link):
        half = blocks.shape[0] // self.cores
        total = blocks[:half] + self.hop(blocks[half:].astype(link), core=-1).astype(F32)
        quarter = half // self.second
        m = quarter // self.first
        acc = None
        for r in reversed(range(self.first)):
            piece = None
            for xx in reversed(range(self.second)):
                part = total[xx * quarter + r * m : xx * quarter + (r + 1) * m]
                if piece is not None:
                    part = part + self.hop(piece.astype(link), second=-1).astype(F32)
                piece = part
            if acc is not None:
                piece = piece + self.hop(acc.astype(link), first=-1).astype(F32)
            acc = piece
        return acc

    def scatter_small(self, blocks):
        half = blocks.shape[0] // self.cores
        total = blocks[:half] + self.hop(blocks[half:], core=-1)
        quarter = half // self.second
        acc = total[half - quarter :]
        for xx in reversed(range(self.second - 1)):
            acc = total[xx * quarter : (xx + 1) * quarter] + self.hop(acc, second=-1)
        m = quarter // self.first
        result = acc[:m]
        for r in range(1, self.first):
            result = result + self.hop(acc[r * m : (r + 1) * m], first=-r)
        return result


class Pair:
    def __init__(self, n_tensor):
        self.size = n_tensor

    def swap(self, value):
        return lax.ppermute(value, "tensor", [(0, 1), (1, 0)])

    def spread(self, own):
        if self.size != 2:
            return lax.all_gather(own, "tensor", axis=0, tiled=True)
        other = self.swap(own)
        first = lax.axis_index("tensor") == 0
        return jnp.concatenate(
            [jnp.where(first, own, other), jnp.where(first, other, own)], axis=0
        )

    def total(self, partial_rows):
        rounded = partial_rows.astype(BF16)
        if self.size != 2:
            return lax.psum(rounded.astype(F32), "tensor")
        return rounded.astype(F32) + self.swap(rounded).astype(F32)

    def collect(self, partial_rows):
        rounded = partial_rows.astype(BF16)
        if self.size != 2:
            return lax.psum_scatter(rounded, "tensor", scatter_dimension=0, tiled=True).astype(F32)
        rows = rounded.shape[0] // 2
        index = lax.axis_index("tensor")
        away = lax.dynamic_slice_in_dim(rounded, (1 - index) * rows, rows, 0)
        stay = lax.dynamic_slice_in_dim(rounded, index * rows, rows, 0)
        return stay.astype(F32) + self.swap(away).astype(F32)

    def collect_small(self, terms):
        if self.size != 2:
            return lax.psum_scatter(terms, "tensor", scatter_dimension=0, tiled=True)[0]
        index = lax.axis_index("tensor")
        return terms[index] + self.swap(terms[1 - index])

    def own(self, rows_all):
        rows = rows_all.shape[0] // self.size
        return lax.dynamic_slice_in_dim(rows_all, lax.axis_index("tensor") * rows, rows, 0)


def layer(n_fsdp, n_tensor):
    ring = Ring(n_fsdp)
    pair = Pair(n_tensor)

    def shards(
        tokens,
        segments,
        norm_gains,
        row_biases,
        attention_in,
        query_bias,
        value_bias,
        attention_out,
        hidden_in,
        hidden_bias,
        hidden_out,
        output_grad,
    ):
        m = attention_in.shape[0]
        model_width = m * n_fsdp
        local_width = attention_in.shape[2]
        heads = query_bias.shape[0]
        hidden_width = hidden_in.shape[1]
        seq_count, seq_len = segments.shape
        head_shape = (seq_count, seq_len, heads, HD)
        score_scale = 1.0 / math.sqrt(HD)
        q_len, h_len = query_bias.size, hidden_bias.size

        in_full = ring.gather(attention_in.reshape(m, 3 * local_width))
        out_t = ring.gather(attention_out.T)
        up_full = ring.gather(hidden_in)
        down_t = ring.gather(hidden_out.T)

        rows_six = jnp.concatenate([norm_gains, row_biases], axis=0)
        six_all = pair.spread(rows_six[None])
        six_all = six_all.transpose(1, 0, 2).reshape(1, 6 * m)
        flat = jnp.concatenate(
            [
                six_all,
                query_bias.astype(F32).reshape(1, q_len),
                value_bias.astype(F32).reshape(1, q_len),
                hidden_bias.astype(F32).reshape(1, h_len),
            ],
            axis=1,
        )
        small = ring.gather_small(flat)
        six_full = (
            small[:, : 6 * m].reshape(n_fsdp, 6, m).transpose(1, 0, 2).reshape(6, model_width)
        )
        gains_all, biases_all = six_full[:2], six_full[2:]
        block_ids = ring.local_block(jnp.arange(n_fsdp))
        to_global = (block_ids[:, None] == jnp.arange(n_fsdp)[None, :]).astype(BF16)
        head_small = dot(to_global, small[:, 6 * m :].astype(BF16), ((1,), (0,)))

        def head_row(start, length, width):
            return (
                head_small[:, start : start + length]
                .reshape(n_fsdp, heads, length // heads)
                .transpose(1, 0, 2)
                .reshape(width)
            )

        query_add = head_row(0, q_len, local_width)
        value_add = head_row(q_len, q_len, local_width)
        hidden_add = head_row(2 * q_len, h_len, hidden_width)

        places = jnp.arange(model_width)
        local_places = ring.local_block(places // m) * m + places % m
        to_local = (local_places[:, None] == places[None, :]).astype(BF16)
        tok_b = dot(pair.spread(tokens), to_local, ((1,), (0,))).astype(BF16)
        grad_all = dot(pair.spread(output_grad), to_local, ((1,), (0,))).astype(BF16)
        tok_rows = tok_b.astype(F32)
        grad_rows = grad_all.astype(F32)

        allowed = pair_mask(segments)
        normed_one, inverse_one = normalize(tok_rows)
        in_one = (normed_one * gains_all[0] + biases_all[0]).astype(BF16)
        projected = dot(in_one, in_full, ((1,), (0,)))
        query_rows = (projected[:, :local_width] + query_add).astype(BF16).reshape(head_shape)
        key_rows = projected[:, local_width : 2 * local_width].astype(BF16).reshape(head_shape)
        value_rows = (projected[:, 2 * local_width :] + value_add).astype(BF16).reshape(head_shape)
        mixed, log_total = attend(query_rows, key_rows, value_rows, allowed, score_scale)
        mixed_rows = mixed.reshape(-1, local_width).astype(BF16)
        attn_rows = pair.total(dot(mixed_rows, out_t, ((1,), (1,))))
        resid_rows = tok_rows + attn_rows + biases_all[1]
        normed_two, inverse_two = normalize(resid_rows)
        in_two = (normed_two * gains_all[1] + biases_all[2]).astype(BF16)
        pre_act = dot(in_two, up_full, ((1,), (0,))) + hidden_add
        act, slope = gelu_parts(pre_act)
        act_rows = act.astype(BF16)

        g_pre = dot(grad_all, down_t, ((1,), (0,))) * slope
        g_hidden_add = jnp.sum(g_pre, axis=0)
        g_pre_b = g_pre.astype(BF16)
        g_two_part = dot(g_pre_b, up_full, ((1,), (1,)))
        g_norm_two = pair.total(g_two_part)
        g_down_t = ring.scatter(dot(grad_all, act_rows, ((0,), (0,))), BF16)
        g_up = ring.scatter(dot(in_two, g_pre_b, ((0,), (0,))), BF16)

        mlp_rows = pair.collect(dot(act_rows, down_t, ((1,), (1,))))
        result = (pair.own(resid_rows) + mlp_rows + biases_all[3]).astype(BF16)
        result = dot(result, to_local, ((1,), (1,))).astype(BF16)

        g_resid = grad_rows + normalize_back(g_norm_two, normed_two, inverse_two, gains_all[1])
        g_resid_b = g_resid.astype(BF16)
        g_out_t = ring.scatter(dot(g_resid_b, mixed_rows, ((0,), (0,))), BF16)
        g_mixed = dot(g_resid_b, out_t, ((1,), (0,))).astype(BF16).reshape(head_shape)
        g_query, g_keys, g_values = attend_back(
            query_rows, key_rows, value_rows, allowed, score_scale, log_total, g_mixed
        )
        g_query = g_query.reshape(-1, local_width)
        g_keys = g_keys.reshape(-1, local_width)
        g_values = g_values.reshape(-1, local_width)
        g_query_add = jnp.sum(g_query, axis=0)
        g_value_add = jnp.sum(g_values, axis=0)
        g_proj = jnp.concatenate([g_query, g_keys, g_values], axis=1).astype(BF16)
        g_in = ring.scatter(dot(in_one, g_proj, ((0,), (0,))), BF16)
        g_one_part = dot(g_proj, in_full, ((1,), (1,)))
        g_norm_one = pair.collect(g_one_part)
        tokens_grad = (
            pair.own(g_resid)
            + normalize_back(g_norm_one, pair.own(normed_one), pair.own(inverse_one), gains_all[0])
        ).astype(BF16)
        tokens_grad = dot(tokens_grad, to_local, ((1,), (1,))).astype(BF16)

        own_grad = pair.own(grad_rows)
        six_terms = jnp.stack(
            [
                jnp.sum(g_one_part * normed_one, axis=0),
                jnp.sum(g_two_part * normed_two, axis=0),
                jnp.sum(g_one_part, axis=0),
                jnp.sum(pair.own(g_resid), axis=0),
                jnp.sum(g_two_part, axis=0),
                jnp.sum(own_grad, axis=0),
            ]
        )
        six_terms = six_terms.reshape(6, n_fsdp, m).transpose(1, 0, 2).reshape(n_fsdp, 6 * m)

        def head_blocks(row, length):
            return (
                row.reshape(heads, n_fsdp, length // heads)
                .transpose(1, 0, 2)
                .reshape(n_fsdp, length)
            )

        head_terms = jnp.concatenate(
            [
                head_blocks(g_query_add, q_len),
                head_blocks(g_value_add, q_len),
                head_blocks(g_hidden_add, h_len),
            ],
            axis=1,
        )
        head_terms = lax.dot_general(
            to_global.astype(F32),
            head_terms,
            (((0,), (0,)), ((), ())),
            precision=lax.Precision.HIGHEST,
            preferred_element_type=F32,
        )
        sums = ring.scatter_small(jnp.concatenate([six_terms, head_terms], axis=1))[0]
        six_sum = sums[: 6 * m].reshape(6, n_tensor, m // n_tensor).transpose(1, 0, 2)
        six_sum = pair.collect_small(six_sum)
        head_sum = sums[6 * m :]
        return (
            result,
            tokens_grad,
            g_in.reshape(m, 3, local_width),
            g_out_t.T,
            g_up,
            g_down_t.T,
            head_sum[:q_len].reshape(query_bias.shape),
            head_sum[q_len : 2 * q_len].reshape(value_bias.shape),
            head_sum[2 * q_len :].reshape(hidden_bias.shape),
            six_sum[:2],
            six_sum[2:],
        )

    return shards


def solution(mesh):
    n_fsdp = mesh.shape["fsdp"]
    n_tensor = mesh.shape["tensor"]
    rows = P(("fsdp", "tensor"), None)
    columns = P(None, ("fsdp", "tensor"))
    head = P("tensor", "fsdp")
    into = P("fsdp", None, "tensor")
    up = P("fsdp", "tensor")
    return jax.shard_map(
        layer(n_fsdp, n_tensor),
        mesh=mesh,
        in_specs=(
            rows,
            P("fsdp", None),
            columns,
            columns,
            into,
            head,
            head,
            head,
            up,
            head,
            head,
            rows,
        ),
        out_specs=(rows, rows, into, head, up, head, head, head, head, columns, columns),
        check_vma=False,
    )
```

```python
import math

import jax
import jax.numpy as jnp
import numpy as np
from jax import lax
from jax.experimental import pallas as pl
from jax.experimental.pallas import tpu as pltpu
from jax.sharding import PartitionSpec as P

HD = 64
EPS = 1e-05
GELU_C = math.sqrt(2.0 / math.pi)
GELU_A = 0.044715
MASKED = -1e30
BF16 = jnp.bfloat16
F32 = jnp.float32
VMEM_LIMIT = 48 * 1024 * 1024


def gelu_parts(pre_act):
    square = pre_act * pre_act
    tanh_part = jnp.tanh(GELU_C * pre_act * (1.0 + GELU_A * square))
    half = 0.5 * (1.0 + tanh_part)
    slope = half + 0.5 * pre_act * (1.0 - tanh_part * tanh_part) * GELU_C * (
        1.0 + 3.0 * GELU_A * square
    )
    return pre_act * half, slope


def normalize(row_data):
    row_mean = jnp.mean(row_data, axis=-1, keepdims=True)
    centered = row_data - row_mean
    variance = jnp.mean(centered * centered, axis=-1, keepdims=True)
    inverse = lax.rsqrt(variance + EPS)
    return centered * inverse, inverse


def normalize_back(grad_rows, normed, inverse, gain_row):
    scaled = grad_rows * gain_row
    return inverse * (
        scaled
        - jnp.mean(scaled, axis=-1, keepdims=True)
        - normed * jnp.mean(scaled * normed, axis=-1, keepdims=True)
    )


def tie(*values):
    return lax.optimization_barrier(values)


def assemble(pieces):
    m, n = pieces[0].shape
    count = len(pieces)

    def copy(*refs):
        for i in range(count):
            refs[count][i * m : (i + 1) * m, :] = refs[i][...]

    return pl.pallas_call(
        copy,
        out_shape=jax.ShapeDtypeStruct((count * m, n), pieces[0].dtype),
        compiler_params=pltpu.CompilerParams(vmem_limit_bytes=VMEM_LIMIT),
        name="assemble",
    )(*pieces)


def ring_add(sums, k, chips, side, arrived):
    count = len(sums)
    m = sums[0].shape[0] // chips
    widths = [own.shape[1] for own in sums]

    def add(*refs):
        target, start = refs[-1], 0
        for i in range(count):
            size = m if side == 0 else widths[i]
            part = slice(start, start + size)
            at = (part, slice(None)) if side == 0 else (slice(None), part)
            value = refs[i][...]
            if arrived is not None:
                value = (value.astype(F32) + refs[count][at].astype(F32)).astype(BF16)
            target[at] = value
            start += size

    shape = (count * m, widths[0]) if side == 0 else (m, sum(widths))
    blocks = [pl.BlockSpec((m, n), lambda i: (k, 0)) for n in widths]
    whole = pl.BlockSpec(shape, lambda i: (0, 0))
    given = [] if arrived is None else [arrived]
    return pl.pallas_call(
        add,
        grid=(1,),
        in_specs=blocks + [whole] * len(given),
        out_specs=whole,
        out_shape=jax.ShapeDtypeStruct(shape, BF16),
        name="ring_add",
    )(*sums, *given)


def probabilities(query, key, allowed, score_scale):
    scores = dot(query, key, ((1,), (1,))) * score_scale
    scores = jnp.where(allowed, scores, MASKED)
    terms = jnp.exp(scores - jnp.max(scores, axis=-1, keepdims=True))
    return terms / jnp.sum(terms, axis=-1, keepdims=True)


def allowed_pairs(segment_column, segment_row):
    seq_len = segment_row.shape[1]
    causal = lax.broadcasted_iota(jnp.int32, (seq_len, seq_len), 0) >= lax.broadcasted_iota(
        jnp.int32, (seq_len, seq_len), 1
    )
    return causal & (segment_column == segment_row)


def attend(query_rows, key_rows, value_rows, segments, score_scale):
    seq_count, seq_len = segments.shape
    width = query_rows.shape[1]
    step = min(width, 2 * HD)

    def forward(column, row, query, key, value, mixed):
        allowed = allowed_pairs(column[...], row[0])
        for h in range(step // HD):
            at = slice(h * HD, (h + 1) * HD)
            probs = probabilities(query[:, at], key[:, at], allowed, score_scale)
            mixed[:, at] = dot(probs.astype(BF16), value[:, at], ((1,), (0,))).astype(BF16)

    rows = pl.BlockSpec((seq_len, step), lambda i, j: (i, j))
    return pl.pallas_call(
        forward,
        grid=(seq_count, width // step),
        in_specs=[
            pl.BlockSpec((seq_len, 1), lambda i, j: (i, 0)),
            pl.BlockSpec((1, 1, seq_len), lambda i, j: (i, 0, 0)),
            rows,
            rows,
            rows,
        ],
        out_specs=rows,
        out_shape=jax.ShapeDtypeStruct(query_rows.shape, BF16),
        compiler_params=pltpu.CompilerParams(vmem_limit_bytes=VMEM_LIMIT),
        name="attend",
    )(
        segments.reshape(-1, 1),
        segments.reshape(seq_count, 1, seq_len),
        query_rows,
        key_rows,
        value_rows,
    )


def attend_back(query_rows, key_rows, value_rows, g_mixed, segments, score_scale):
    seq_count, seq_len = segments.shape
    width = query_rows.shape[1]
    step = min(width, 2 * HD)

    def backward(column, row, query, key, value, grad, g_query, g_key, g_value, sum_q, sum_v):
        allowed = allowed_pairs(column[...], row[0])
        for h in range(step // HD):
            at = slice(h * HD, (h + 1) * HD)
            q, k, v, g = query[:, at], key[:, at], value[:, at], grad[:, at]
            probs = probabilities(q, k, allowed, score_scale)
            gv = dot(probs.astype(BF16), g, ((0,), (0,)))
            g_probs = dot(g, v, ((1,), (1,)))
            inner = jnp.sum(probs * g_probs, axis=-1, keepdims=True)
            g_scores = (probs * (g_probs - inner) * score_scale).astype(BF16)
            gq = dot(g_scores, k, ((1,), (0,)))
            g_query[:, at] = gq.astype(BF16)
            g_key[:, at] = dot(g_scores, q, ((0,), (0,))).astype(BF16)
            g_value[:, at] = gv.astype(BF16)
            sum_q[0, :, at] = jnp.sum(gq, axis=0, keepdims=True)
            sum_v[0, :, at] = jnp.sum(gv, axis=0, keepdims=True)

    rows = pl.BlockSpec((seq_len, step), lambda i, j: (i, j))
    sums = pl.BlockSpec((1, 1, step), lambda i, j: (i, 0, j))
    wide = jax.ShapeDtypeStruct(query_rows.shape, BF16)
    total = jax.ShapeDtypeStruct((seq_count, 1, width), F32)
    return pl.pallas_call(
        backward,
        grid=(seq_count, width // step),
        in_specs=[
            pl.BlockSpec((seq_len, 1), lambda i, j: (i, 0)),
            pl.BlockSpec((1, 1, seq_len), lambda i, j: (i, 0, 0)),
            rows,
            rows,
            rows,
            rows,
        ],
        out_specs=[rows, rows, rows, sums, sums],
        out_shape=[wide, wide, wide, total, total],
        compiler_params=pltpu.CompilerParams(vmem_limit_bytes=VMEM_LIMIT),
        name="attend_back",
    )(
        segments.reshape(-1, 1),
        segments.reshape(seq_count, 1, seq_len),
        query_rows,
        key_rows,
        value_rows,
        g_mixed,
    )


def dot(left, right, dims):
    return lax.dot_general(left, right, (dims, ((), ())), preferred_element_type=F32)


def exact_dot(left, right, dims):
    return lax.dot_general(
        left,
        right,
        (dims, ((), ())),
        precision=lax.Precision.HIGHEST,
        preferred_element_type=F32,
    )


class Ring:
    def __init__(self, n_fsdp):
        self.size = n_fsdp
        self.cores = 2
        self.chips = n_fsdp // self.cores
        self.second = n_fsdp // 8
        self.first = self.chips // self.second
        cycle = [(a, 0) for a in range(self.first)]
        for a in reversed(range(self.first)):
            across = list(range(1, self.second))
            cycle += [(a, b) for b in (across if a % 2 else reversed(across))]
        self.cycle = cycle
        self.place = np.zeros(self.chips, np.int32)
        for p, (a, b) in enumerate(cycle):
            self.place[a * self.second + b] = p

    def split(self, index):
        return (
            index // (self.second * self.cores),
            (index // self.cores) % self.second,
            index % self.cores,
        )

    def hop(self, value, first=0, second=0, core=0, along=0):
        pairs = []
        for source in range(self.size):
            a, b, c = self.split(source)
            if along:
                a, b = self.cycle[(self.place[a * self.second + b] + along) % self.chips]
            a, b, c = (a + first) % self.first, (b + second) % self.second, (c + core) % self.cores
            pairs.append((source, (a * self.second + b) * self.cores + c))
        return lax.ppermute(value, "fsdp", pairs)

    def grid_number(self):
        a, b, c = self.split(lax.axis_index("fsdp"))
        ga, gb, gc = self.split(np.arange(self.size))
        r = (a - ga + self.first) % self.first
        xx = (b - gb + self.second) % self.second
        cc = (c - gc + self.cores) % self.cores
        return (cc * self.second + xx) * self.first + r

    def cycle_number(self, blocks):
        index = lax.axis_index("fsdp")
        own = jnp.asarray(self.place)[index // self.cores]
        k = (own - self.place[blocks // self.cores] + self.chips) % self.chips
        cc = (index + blocks) % self.cores
        return cc * self.chips + k

    def gather_small(self, block):
        own = [block] + [self.hop(block, first=r) for r in range(1, self.first)]
        current = own = jnp.concatenate(own, axis=0)
        for _ in range(self.second - 1):
            current = self.hop(current, second=1)
            own = jnp.concatenate([own, current], axis=0)
        return jnp.concatenate([own, self.hop(own, core=1)], axis=0)

    def scatter_small(self, blocks):
        half = blocks.shape[0] // self.cores
        total = blocks[:half] + self.hop(blocks[half:], core=-1)
        quarter = half // self.second
        acc = total[half - quarter :]
        for xx in reversed(range(self.second - 1)):
            acc = total[xx * quarter : (xx + 1) * quarter] + self.hop(acc, second=-1)
        m = quarter // self.first
        result = acc[:m]
        for r in range(1, self.first):
            result = result + self.hop(acc[r * m : (r + 1) * m], first=-r)
        return result


class Gather:
    def __init__(self, ring, block):
        self.ring = ring
        self.up, self.down = [block], [block]

    def step(self):
        if len(self.up) <= self.ring.chips // 2:
            self.up.append(self.ring.hop(self.up[-1], along=1))
        if len(self.down) <= (self.ring.chips - 1) // 2:
            self.down.append(self.ring.hop(self.down[-1], along=-1))

    def steps(self, count):
        for _ in range(count):
            self.step()

    def tied(self, *values):
        up, down, *values = tie(self.up[-1], self.down[-1], *values)
        if len(self.up) > 1:
            self.up[-1] = up
            self.down[-1] = down
        return values if len(values) > 1 else values[0]

    def whole(self):
        while len(self.up) <= self.ring.chips // 2:
            self.step()
        own = self.up + self.down[:0:-1]
        return assemble(own + [self.ring.hop(piece, core=1) for piece in own])


class Scatter:
    def __init__(self, ring, side):
        self.ring, self.side, self.sums = ring, side, []
        self.up = self.down = None
        self.done = 0

    def away(self, left, right):
        half = left.shape[1] // self.ring.cores
        moved = dot(left[:, half:], right, ((0,), (0,))).astype(BF16)
        return self.ring.hop(moved, core=-1)

    def add(self, left, right, arrived):
        half = left.shape[1] // self.ring.cores
        own = dot(left[:, :half], right, ((0,), (0,))) + arrived.astype(F32)
        self.sums.append(own.astype(BF16))

    def step(self):
        chips = self.ring.chips
        k = chips // 2 - self.done
        if k >= 1:
            self.up = self.ring.hop(ring_add(self.sums, k, chips, self.side, self.up), along=-1)
        k = chips // 2 + 1 + self.done
        if k < chips:
            self.down = self.ring.hop(ring_add(self.sums, k, chips, self.side, self.down), along=1)
        self.done += 1

    def tied(self, *values):
        self.up, self.down, *values = tie(self.up, self.down, *values)
        return values if len(values) > 1 else values[0]

    def totals(self):
        chips = self.ring.chips
        while self.done < chips // 2:
            self.step()
        arrived = self.up.astype(F32) + self.down.astype(F32)
        totals, start = [], 0
        for own in self.sums:
            m, n = own.shape[0] // chips, own.shape[1]
            part = arrived[start : start + m] if self.side == 0 else arrived[:, start : start + n]
            totals.append(own[:m].astype(F32) + part)
            start += m if self.side == 0 else n
        return totals


class Pair:
    def __init__(self, n_tensor):
        self.size = n_tensor

    def swap(self, value):
        return lax.ppermute(value, "tensor", [(0, 1), (1, 0)])

    def spread(self, own):
        if self.size != 2:
            return lax.all_gather(own, "tensor", axis=0, tiled=True)
        other = self.swap(own)
        first = lax.axis_index("tensor") == 0
        return jnp.concatenate(
            [jnp.where(first, own, other), jnp.where(first, other, own)], axis=0
        )

    def total(self, partial_rows):
        rounded = partial_rows.astype(BF16)
        if self.size != 2:
            return lax.psum(rounded.astype(F32), "tensor")
        return rounded.astype(F32) + self.swap(rounded).astype(F32)

    def collect(self, partial_rows):
        rounded = partial_rows.astype(BF16)
        if self.size != 2:
            return lax.psum_scatter(rounded, "tensor", scatter_dimension=0, tiled=True).astype(F32)
        rows = rounded.shape[0] // 2
        index = lax.axis_index("tensor")
        away = lax.dynamic_slice_in_dim(rounded, (1 - index) * rows, rows, 0)
        stay = lax.dynamic_slice_in_dim(rounded, index * rows, rows, 0)
        return stay.astype(F32) + self.swap(away).astype(F32)

    def collect_small(self, terms):
        if self.size != 2:
            return lax.psum_scatter(terms, "tensor", scatter_dimension=0, tiled=True)[0]
        index = lax.axis_index("tensor")
        return terms[index] + self.swap(terms[1 - index])

    def own(self, rows_all):
        rows = rows_all.shape[0] // self.size
        return lax.dynamic_slice_in_dim(rows_all, lax.axis_index("tensor") * rows, rows, 0)


def layer(n_fsdp, n_tensor):
    ring = Ring(n_fsdp)
    pair = Pair(n_tensor)

    def shards(
        tokens,
        segments,
        norm_gains,
        row_biases,
        attention_in,
        query_bias,
        value_bias,
        attention_out,
        hidden_in,
        hidden_bias,
        hidden_out,
        output_grad,
    ):
        m = attention_in.shape[0]
        model_width = m * n_fsdp
        local_width = attention_in.shape[2]
        heads = query_bias.shape[0]
        hidden_width = hidden_in.shape[1]
        score_scale = 1.0 / math.sqrt(HD)
        q_len, h_len = query_bias.size, hidden_bias.size

        rows_six = jnp.concatenate([norm_gains, row_biases], axis=0)
        six_all = pair.spread(rows_six[None])
        six_all = six_all.transpose(1, 0, 2).reshape(1, 6 * m)
        flat = jnp.concatenate(
            [
                six_all,
                query_bias.astype(F32).reshape(1, q_len),
                value_bias.astype(F32).reshape(1, q_len),
                hidden_bias.astype(F32).reshape(1, h_len),
            ],
            axis=1,
        )
        small = ring.gather_small(flat)
        numbers = np.arange(n_fsdp)
        from_grid = (ring.grid_number()[:, None] == numbers[None, :]).astype(F32)
        from_cycle = (ring.cycle_number(numbers)[:, None] == numbers[None, :]).astype(F32)
        small_global = exact_dot(from_grid, small, ((1,), (0,)))
        six_full = exact_dot(from_cycle, small_global[:, : 6 * m], ((0,), (0,)))
        six_full = six_full.reshape(n_fsdp, 6, m).transpose(1, 0, 2).reshape(6, model_width)
        gains_all, biases_all = six_full[:2], six_full[2:]
        head_small = small_global[:, 6 * m :]

        def head_row(start, length, width):
            return (
                head_small[:, start : start + length]
                .reshape(n_fsdp, heads, length // heads)
                .transpose(1, 0, 2)
                .reshape(width)
            )

        query_add = head_row(0, q_len, local_width)
        value_add = head_row(q_len, q_len, local_width)
        hidden_add = head_row(2 * q_len, h_len, hidden_width)

        places = np.arange(model_width)
        local_places = ring.cycle_number(places // m) * m + places % m
        to_local = (local_places[:, None] == places[None, :]).astype(BF16)
        tok_b = dot(pair.spread(tokens), to_local, ((1,), (0,))).astype(BF16)
        tok_rows = tok_b.astype(F32)
        normed_one, inverse_one = normalize(tok_rows)
        in_one = (normed_one * gains_all[0] + biases_all[0]).astype(BF16)

        half_way = ring.chips // 2
        one = Gather(
            ring,
            jnp.concatenate([attention_in.reshape(m, 3 * local_width), attention_out.T], axis=1),
        )
        one.steps(half_way - 1)
        up = Gather(ring, one.tied(hidden_in))
        one_full = one.whole()
        up.step()
        in_full, out_t = one_full[:, : 3 * local_width], one_full[:, 3 * local_width :]
        projected = dot(in_one, in_full, ((1,), (0,)))
        query_rows = (projected[:, :local_width] + query_add).astype(BF16)
        key_rows = projected[:, local_width : 2 * local_width].astype(BF16)
        value_rows = (projected[:, 2 * local_width :] + value_add).astype(BF16)
        query_rows, down_block, output_grad = up.tied(query_rows, hidden_out.T, output_grad)
        up.step()
        down = Gather(ring, down_block)
        down.step()
        grad_all = dot(pair.spread(output_grad), to_local, ((1,), (0,))).astype(BF16)
        mixed_rows = attend(query_rows, key_rows, value_rows, segments, score_scale)
        mixed_rows = down.tied(up.tied(mixed_rows))
        attn_rows = pair.total(dot(mixed_rows, out_t, ((1,), (1,))))
        up.steps(half_way - 2)
        down.steps(half_way - 2)
        attn_rows = down.tied(up.tied(attn_rows))
        resid_rows = tok_rows + attn_rows + biases_all[1]
        normed_two, inverse_two = normalize(resid_rows)
        in_two = (normed_two * gains_all[1] + biases_all[2]).astype(BF16)
        up_full = up.whole()
        pre_act = dot(in_two, up_full, ((1,), (0,))) + hidden_add
        act, slope = gelu_parts(pre_act)
        act_rows = act.astype(BF16)
        down_t = down.whole()

        g_pre = dot(grad_all, down_t, ((1,), (0,))) * slope
        g_hidden_add = jnp.sum(g_pre, axis=0)
        g_pre_b = g_pre.astype(BF16)
        g_two_part = dot(g_pre_b, up_full, ((1,), (1,)))
        g_norm_two = pair.total(g_two_part)
        hidden = Scatter(ring, 0)
        down_away = hidden.away(grad_all, act_rows)
        up_away = hidden.away(in_two, g_pre_b)
        hidden.add(grad_all, act_rows, down_away)
        hidden.add(in_two, g_pre_b, up_away)
        hidden.step()

        mlp_rows = pair.collect(dot(act_rows, down_t, ((1,), (1,))))
        result = (pair.own(resid_rows) + mlp_rows + biases_all[3]).astype(BF16)
        result = dot(result, to_local, ((1,), (1,))).astype(BF16)

        grad_rows = grad_all.astype(F32)
        g_norm_two = hidden.tied(g_norm_two)
        hidden.step()
        g_resid = grad_rows + normalize_back(g_norm_two, normed_two, inverse_two, gains_all[1])
        g_resid_b = g_resid.astype(BF16)
        g_mixed = dot(g_resid_b, out_t, ((1,), (0,))).astype(BF16)
        outer = Scatter(ring, 1)
        out_away = outer.away(g_resid_b, mixed_rows)
        g_query, g_keys, g_values, g_query_add, g_value_add = attend_back(
            query_rows, key_rows, value_rows, g_mixed, segments, score_scale
        )
        g_query_add = jnp.sum(g_query_add, axis=0)
        g_value_add = jnp.sum(g_value_add, axis=0)
        g_proj = jnp.concatenate([g_query, g_keys, g_values], axis=1)
        g_proj = hidden.tied(g_proj)
        hidden.step()
        in_away = outer.away(in_one, g_proj)
        in_away = hidden.tied(in_away)
        outer.add(in_one, g_proj, in_away)
        outer.add(g_resid_b, mixed_rows, out_away)
        hidden_sums = hidden.totals()
        g_down_t, g_up = hidden_sums
        g_in, g_out_t = outer.totals()
        g_one_part = dot(g_proj, in_full, ((1,), (1,)))
        g_norm_one = pair.collect(g_one_part)
        tokens_grad = (
            pair.own(g_resid)
            + normalize_back(g_norm_one, pair.own(normed_one), pair.own(inverse_one), gains_all[0])
        ).astype(BF16)
        tokens_grad = dot(tokens_grad, to_local, ((1,), (1,))).astype(BF16)

        own_grad = pair.own(grad_rows)
        six_terms = jnp.stack(
            [
                jnp.sum(g_one_part * normed_one, axis=0),
                jnp.sum(g_two_part * normed_two, axis=0),
                jnp.sum(g_one_part, axis=0),
                jnp.sum(pair.own(g_resid), axis=0),
                jnp.sum(g_two_part, axis=0),
                jnp.sum(own_grad, axis=0),
            ]
        )
        six_terms = six_terms.reshape(6, n_fsdp, m).transpose(1, 0, 2).reshape(n_fsdp, 6 * m)
        six_terms = exact_dot(from_cycle, six_terms, ((1,), (0,)))

        def head_blocks(row, length):
            return (
                row.reshape(heads, n_fsdp, length // heads)
                .transpose(1, 0, 2)
                .reshape(n_fsdp, length)
            )

        head_terms = jnp.concatenate(
            [
                head_blocks(g_query_add, q_len),
                head_blocks(g_value_add, q_len),
                head_blocks(g_hidden_add, h_len),
            ],
            axis=1,
        )
        terms = jnp.concatenate([six_terms, head_terms], axis=1)
        terms = exact_dot(from_grid, terms, ((0,), (0,)))
        sums = ring.scatter_small(terms)[0]
        six_sum = sums[: 6 * m].reshape(6, n_tensor, m // n_tensor).transpose(1, 0, 2)
        six_sum = pair.collect_small(six_sum)
        head_sum = sums[6 * m :]
        return (
            result,
            tokens_grad,
            g_in.reshape(m, 3, local_width),
            g_out_t.T,
            g_up,
            g_down_t.T,
            head_sum[:q_len].reshape(query_bias.shape),
            head_sum[q_len : 2 * q_len].reshape(value_bias.shape),
            head_sum[2 * q_len :].reshape(hidden_bias.shape),
            six_sum[:2],
            six_sum[2:],
        )

    return shards


def solution(mesh):
    n_fsdp = mesh.shape["fsdp"]
    n_tensor = mesh.shape["tensor"]
    rows = P(("fsdp", "tensor"), None)
    columns = P(None, ("fsdp", "tensor"))
    head = P("tensor", "fsdp")
    into = P("fsdp", None, "tensor")
    up = P("fsdp", "tensor")
    return jax.shard_map(
        layer(n_fsdp, n_tensor),
        mesh=mesh,
        in_specs=(
            rows,
            P("fsdp", None),
            columns,
            columns,
            into,
            head,
            head,
            head,
            up,
            head,
            head,
            rows,
        ),
        out_specs=(rows, rows, into, head, up, head, head, head, head, columns, columns),
        check_vma=False,
    )
```

```python
import math

import jax
import jax.numpy as jnp
import numpy as np
from jax import lax
from jax.experimental import pallas as pl
from jax.experimental.pallas import tpu as pltpu
from jax.sharding import PartitionSpec as P

HD = 64
EPS = 1e-05
GELU_C = math.sqrt(2.0 / math.pi)
GELU_A = 0.044715
MASKED = -1e30
BF16 = jnp.bfloat16
F32 = jnp.float32
LANES = 128
VMEM_LIMIT = 48 * 1024 * 1024


def gelu_parts(pre_act):
    square = pre_act * pre_act
    tanh_part = jnp.tanh(GELU_C * pre_act * (1.0 + GELU_A * square))
    half = 0.5 * (1.0 + tanh_part)
    slope = half + 0.5 * pre_act * (1.0 - tanh_part * tanh_part) * GELU_C * (
        1.0 + 3.0 * GELU_A * square
    )
    return pre_act * half, slope


def normalize(row_data):
    row_mean = jnp.mean(row_data, axis=-1, keepdims=True)
    centered = row_data - row_mean
    variance = jnp.mean(centered * centered, axis=-1, keepdims=True)
    inverse = lax.rsqrt(variance + EPS)
    return centered * inverse, inverse


def normalize_back(grad_rows, normed, inverse, gain_row):
    scaled = grad_rows * gain_row
    return inverse * (
        scaled
        - jnp.mean(scaled, axis=-1, keepdims=True)
        - normed * jnp.mean(scaled * normed, axis=-1, keepdims=True)
    )


def tie(*values):
    return lax.optimization_barrier(values)


def assemble(table, pieces):
    m, n = pieces[0].shape
    count = len(pieces)

    def copy(places, *refs):
        for i in range(count):
            refs[count][pl.ds(pl.multiple_of(places[i] * m, m), m), :] = refs[i][...]

    return pl.pallas_call(
        copy,
        in_specs=[pl.BlockSpec(memory_space=pltpu.SMEM)]
        + [pl.BlockSpec(memory_space=pltpu.VMEM)] * count,
        out_shape=jax.ShapeDtypeStruct((count * m, n), pieces[0].dtype),
        compiler_params=pltpu.CompilerParams(vmem_limit_bytes=VMEM_LIMIT),
        name="assemble",
    )(table, *pieces)


def row_blocks(table, sums, at, m, given=None):
    count = len(sums)
    widths = [own.shape[1] for own in sums]

    def read(places, *refs):
        for j, entry in enumerate(at):
            rows = pl.ds(pl.multiple_of(places[entry] * m, m), m)
            start = 0
            for i in range(count):
                spot = (slice(j * m, (j + 1) * m), slice(start, start + widths[i]))
                value = refs[i][rows, :]
                if given is not None:
                    value = (value.astype(F32) + refs[count][spot].astype(F32)).astype(BF16)
                refs[-1][spot] = value
                start += widths[i]

    arrays = [*sums] if given is None else [*sums, given]
    return pl.pallas_call(
        read,
        in_specs=[pl.BlockSpec(memory_space=pltpu.SMEM)]
        + [pl.BlockSpec(memory_space=pltpu.VMEM)] * len(arrays),
        out_shape=jax.ShapeDtypeStruct((len(at) * m, sum(widths)), BF16),
        compiler_params=pltpu.CompilerParams(vmem_limit_bytes=VMEM_LIMIT),
        name="row_blocks",
    )(table, *arrays)


def ring_add(own, numbers, arrived):
    lanes = len(numbers)
    shape = arrived[0].shape

    def add(*refs):
        for j in range(lanes):
            total = refs[j][...].astype(F32) + refs[lanes + j][...].astype(F32)
            refs[2 * lanes + j][...] = total.astype(BF16)

    blocks = [pl.BlockSpec(shape, lambda i, k=k: (k, 0)) for k in numbers]
    whole = pl.BlockSpec(shape, lambda i: (0, 0))
    return pl.pallas_call(
        add,
        grid=(1,),
        in_specs=blocks + [whole] * lanes,
        out_specs=[whole] * lanes,
        out_shape=[jax.ShapeDtypeStruct(shape, BF16)] * lanes,
        name="ring_add",
    )(*[own] * lanes, *arrived)


def paired_products(lefts, rights):
    depth, rows = lefts[0].shape
    width = rights[0].shape[1]
    tile = min(width, 512)
    half = width // tile

    def multiply(left_a, left_b, right_a, right_b, target, turned):
        j = pl.program_id(0)

        @pl.when(j == 0)
        def _():
            turned[...] = left_a[...].T

        @pl.when(j == half)
        def _():
            turned[...] = left_b[...].T

        @pl.when(j < half)
        def _():
            target[...] = dot(turned[...], right_a[...], ((1,), (0,))).astype(BF16)

        @pl.when(j >= half)
        def _():
            target[...] = dot(turned[...], right_b[...], ((1,), (0,))).astype(BF16)

    whole = pl.BlockSpec((depth, rows), lambda j: (0, 0))
    return pl.pallas_call(
        multiply,
        grid=(2 * half,),
        in_specs=[
            whole,
            whole,
            pl.BlockSpec((depth, tile), lambda j: (0, jnp.minimum(j, half - 1))),
            pl.BlockSpec((depth, tile), lambda j: (0, jnp.maximum(j - half, 0))),
        ],
        out_specs=pl.BlockSpec((rows, tile), lambda j: (0, j)),
        out_shape=jax.ShapeDtypeStruct((rows, 2 * width), BF16),
        scratch_shapes=[pltpu.VMEM((rows, depth), BF16)],
        compiler_params=pltpu.CompilerParams(vmem_limit_bytes=VMEM_LIMIT),
        name="paired_products",
    )(*lefts, *rights)


def allowed_pairs(column, row):
    shape = (column.shape[0], row.shape[1])
    causal = lax.broadcasted_iota(jnp.int32, shape, 0) <= lax.broadcasted_iota(jnp.int32, shape, 1)
    return causal & (column == row)


def probabilities(query, key, allowed):
    scores = jnp.where(allowed, dot(key, query, ((1,), (1,))), MASKED)
    terms = jnp.exp(scores - jnp.max(scores, axis=0, keepdims=True))
    return terms * (1.0 / jnp.sum(terms, axis=0, keepdims=True))


def attend(query_rows, key_rows, value_rows, segments, score_scale):
    seq_count, seq_len = segments.shape
    width = query_rows.shape[1]
    step = min(width, 2 * HD)

    def forward(column, row, query, key, value, mixed):
        allowed = allowed_pairs(column[...], row[0])
        for h in range(step // HD):
            at = slice(h * HD, (h + 1) * HD)
            probs = probabilities(query[:, at] * BF16(score_scale), key[:, at], allowed)
            mixed[:, at] = dot(value[:, at], probs.astype(BF16), ((0,), (0,))).T.astype(BF16)

    rows = pl.BlockSpec((seq_len, step), lambda i, j: (i, j))
    return pl.pallas_call(
        forward,
        grid=(seq_count, width // step),
        in_specs=[
            pl.BlockSpec((seq_len, 1), lambda i, j: (i, 0)),
            pl.BlockSpec((1, 1, seq_len), lambda i, j: (i, 0, 0)),
            rows,
            rows,
            rows,
        ],
        out_specs=rows,
        out_shape=jax.ShapeDtypeStruct(query_rows.shape, BF16),
        compiler_params=pltpu.CompilerParams(vmem_limit_bytes=VMEM_LIMIT),
        name="attend",
    )(
        segments.reshape(-1, 1),
        segments.reshape(seq_count, 1, seq_len),
        query_rows,
        key_rows,
        value_rows,
    )


def attend_back(query_rows, key_rows, value_rows, g_mixed, segments, score_scale):
    seq_count, seq_len = segments.shape
    width = query_rows.shape[1]
    step = min(width, 2 * HD)

    def backward(column, row, query, key, value, grad, g_query, g_key, g_value, sum_q, sum_v):
        allowed = allowed_pairs(column[...], row[0])
        for h in range(step // HD):
            at = slice(h * HD, (h + 1) * HD)
            q, k, v, g = query[:, at] * BF16(score_scale), key[:, at], value[:, at], grad[:, at]
            probs = probabilities(q, k, allowed)
            g_probs = dot(v, g, ((1,), (1,)))
            inner = jnp.sum(probs * g_probs, axis=0, keepdims=True)
            g_scores = (probs * (g_probs - inner)).astype(BF16)
            gv = dot(probs.astype(BF16), g, ((1,), (0,)))
            gq = dot(k, g_scores, ((0,), (0,))).T * score_scale
            g_query[:, at] = gq.astype(BF16)
            g_key[:, at] = dot(g_scores, q, ((1,), (0,))).astype(BF16)
            g_value[:, at] = gv.astype(BF16)
            sum_q[0, :, at] = jnp.sum(gq, axis=0, keepdims=True)
            sum_v[0, :, at] = jnp.sum(gv, axis=0, keepdims=True)

    rows = pl.BlockSpec((seq_len, step), lambda i, j: (i, j))
    sums = pl.BlockSpec((1, 1, step), lambda i, j: (i, 0, j))
    wide = jax.ShapeDtypeStruct(query_rows.shape, BF16)
    total = jax.ShapeDtypeStruct((seq_count, 1, width), F32)
    return pl.pallas_call(
        backward,
        grid=(seq_count, width // step),
        in_specs=[
            pl.BlockSpec((seq_len, 1), lambda i, j: (i, 0)),
            pl.BlockSpec((1, 1, seq_len), lambda i, j: (i, 0, 0)),
            rows,
            rows,
            rows,
            rows,
        ],
        out_specs=[rows, rows, rows, sums, sums],
        out_shape=[wide, wide, wide, total, total],
        compiler_params=pltpu.CompilerParams(vmem_limit_bytes=VMEM_LIMIT),
        name="attend_back",
    )(
        segments.reshape(-1, 1),
        segments.reshape(seq_count, 1, seq_len),
        query_rows,
        key_rows,
        value_rows,
        g_mixed,
    )


def dot(left, right, dims):
    return lax.dot_general(left, right, (dims, ((), ())), preferred_element_type=F32)


def pieces_of(value):
    pieces = []
    for _ in range(3):
        piece = lax.reduce_precision(value, 8, 7)
        pieces.append(piece.astype(BF16))
        value = value - piece
    return pieces


class Ring:
    def __init__(self, n_fsdp):
        self.size = n_fsdp
        self.chips = n_fsdp // 2
        second = n_fsdp // 8
        first = self.chips // second
        cycle = [(a, 0) for a in range(first)]
        for a in reversed(range(first)):
            across = list(range(1, second))
            cycle += [(a, b) for b in (across if a % 2 else reversed(across))]
        self.cycle = [a * second + b for a, b in cycle]
        self.place = {chip: p for p, chip in enumerate(self.cycle)}
        rows = []
        for device in range(n_fsdp):
            chip, core = device // 2, device % 2
            back = [self.cycle[(self.place[chip] - k) % self.chips] for k in range(self.chips)]
            rows.append([2 * c + core for c in back] + [2 * c + 1 - core for c in back])
        self.tables = np.asarray(rows, np.int32)

    def table(self):
        return jnp.asarray(self.tables)[lax.axis_index("fsdp")]

    def hop(self, value, core=0, along=0):
        pairs = []
        for source in range(self.size):
            place = (self.place[source // 2] + along) % self.chips
            pairs.append((source, 2 * self.cycle[place] + (source + core) % 2))
        return lax.ppermute(value, "fsdp", pairs)


class Gather:
    def __init__(self, ring, block):
        self.ring = ring
        self.up, self.down = [block], [block]

    def step(self):
        if len(self.up) <= self.ring.chips // 2:
            self.up.append(self.ring.hop(self.up[-1], along=1))
        if len(self.down) <= (self.ring.chips - 1) // 2:
            self.down.append(self.ring.hop(self.down[-1], along=-1))

    def before(self, *values):
        values = tie(*values, self.up[-1], self.down[-1])[: len(values)]
        return values if len(values) > 1 else values[0]

    def whole(self, table):
        while len(self.up) <= self.ring.chips // 2:
            self.step()
        own = self.up + self.down[:0:-1]
        return assemble(table, own + [self.ring.hop(piece, core=1) for piece in own])


class Scatter:
    def __init__(self, ring, table, sums):
        self.ring = ring
        self.chips = ring.chips
        self.widths = [own.shape[1] for own in sums]
        self.m = sums[0].shape[0] // ring.size
        away = row_blocks(table, sums, range(self.chips, 2 * self.chips), self.m)
        arrived = ring.hop(away, core=1)
        self.own = row_blocks(table, sums, range(self.chips), self.m, arrived)
        self.up = self.down = None
        self.done = 0

    def step(self):
        numbers = [self.chips // 2 - self.done]
        if self.chips // 2 + 1 + self.done < self.chips:
            numbers.append(self.chips // 2 + 1 + self.done)
        if self.done:
            moved = ring_add(self.own, numbers, [self.up, self.down][: len(numbers)])
        else:
            moved = [self.own[k * self.m : (k + 1) * self.m] for k in numbers]
        self.up = self.ring.hop(moved[0], along=-1)
        if len(numbers) > 1:
            self.down = self.ring.hop(moved[1], along=1)
        self.done += 1

    def before(self, *values):
        values = tie(*values, self.up, self.down)[: len(values)]
        return values if len(values) > 1 else values[0]

    def totals(self):
        while self.done < self.chips // 2:
            self.step()
        total = self.own[: self.m].astype(F32) + self.up.astype(F32) + self.down.astype(F32)
        ends = np.cumsum(self.widths)
        return [total[:, end - n : end] for n, end in zip(self.widths, ends)]


class Pair:
    def __init__(self, n_tensor):
        self.size = n_tensor

    def swap(self, value):
        return lax.ppermute(value, "tensor", [(0, 1), (1, 0)])

    def spread(self, own):
        if self.size != 2:
            return lax.all_gather(own, "tensor", axis=0, tiled=True)
        other = self.swap(own)
        first = lax.axis_index("tensor") == 0
        return jnp.concatenate(
            [jnp.where(first, own, other), jnp.where(first, other, own)], axis=0
        )

    def total(self, partial_rows):
        rounded = partial_rows.astype(BF16)
        if self.size != 2:
            return lax.psum(rounded.astype(F32), "tensor")
        return rounded.astype(F32) + self.swap(rounded).astype(F32)

    def collect(self, partial_rows):
        rounded = partial_rows.astype(BF16)
        if self.size != 2:
            return lax.psum_scatter(rounded, "tensor", scatter_dimension=0, tiled=True).astype(F32)
        rows = rounded.shape[0] // 2
        index = lax.axis_index("tensor")
        away = lax.dynamic_slice_in_dim(rounded, (1 - index) * rows, rows, 0)
        stay = lax.dynamic_slice_in_dim(rounded, index * rows, rows, 0)
        return stay.astype(F32) + self.swap(away).astype(F32)

    def sum(self, terms):
        if self.size != 2:
            return lax.psum(terms, "tensor")
        return terms + self.swap(terms)

    def own(self, rows_all):
        rows = rows_all.shape[0] // self.size
        return lax.dynamic_slice_in_dim(rows_all, lax.axis_index("tensor") * rows, rows, 0)


def layer(n_fsdp, n_tensor):
    ring = Ring(n_fsdp)
    pair = Pair(n_tensor)

    def shards(
        tokens,
        segments,
        norm_gains,
        row_biases,
        attention_in,
        query_bias,
        value_bias,
        attention_out,
        hidden_in,
        hidden_bias,
        hidden_out,
        output_grad,
    ):
        m = attention_in.shape[0]
        model_width = m * n_fsdp
        local_width = attention_in.shape[2]
        heads = query_bias.shape[0]
        hidden_width = hidden_in.shape[1]
        score_scale = 1.0 / math.sqrt(HD)
        q_len, h_len = query_bias.size, hidden_bias.size

        table = ring.table()
        six = pair.spread(jnp.concatenate([norm_gains, row_biases], axis=0).T)
        head_flat = jnp.concatenate(
            [query_bias.reshape(q_len), value_bias.reshape(q_len), hidden_bias.reshape(h_len)]
        )
        head_count = -(-head_flat.size // m)
        head_flat = jnp.pad(head_flat, (0, head_count * m - head_flat.size))
        columns = jnp.concatenate(
            pieces_of(six) + [head_flat.reshape(head_count, m).T],
            axis=1,
        )
        columns = jnp.pad(columns, ((0, 0), (0, LANES - columns.shape[1])))
        one = Gather(
            ring,
            jnp.concatenate(
                [attention_in.reshape(m, 3 * local_width), attention_out.T, columns], axis=1
            ),
        )
        one.step()
        hidden_block = jnp.concatenate([hidden_in, hidden_out.T], axis=1)
        hidden_block = one.before(hidden_block)
        hidden_full = lax.all_gather(hidden_block, "fsdp", axis=0, tiled=True)
        up_full, down_t = hidden_full[:, :hidden_width], hidden_full[:, hidden_width:]
        one.step()
        tok_rows = pair.spread(one.before(tokens)).astype(F32)
        one.step()
        grad_all = pair.spread(one.before(output_grad))
        normed_one, inverse_one = normalize(tok_rows)
        one_full = one.whole(table)
        in_full = one_full[:, : 3 * local_width]
        out_t = one_full[:, 3 * local_width : 4 * local_width]
        columns = one_full[:, 4 * local_width :]
        lanes = np.arange(LANES)[None, :]
        is_six = (lanes < 18) & (lanes % 6 == np.arange(6)[:, None])
        is_head = lanes == 18 + np.arange(head_count)[:, None]
        picked = np.concatenate([is_six, is_head], axis=0)
        picked = dot(jnp.asarray(picked, BF16), columns, ((1,), (1,)))
        gains_all, biases_all = picked[:2], picked[2:6]
        head_small = picked[6:].reshape(head_count, n_fsdp, m).transpose(1, 0, 2)
        head_small = head_small.reshape(n_fsdp, head_count * m)

        def head_row(start, length, width):
            return (
                head_small[:, start : start + length]
                .reshape(n_fsdp, heads, length // heads)
                .transpose(1, 0, 2)
                .reshape(width)
            )

        query_add = head_row(0, q_len, local_width)
        value_add = head_row(q_len, q_len, local_width)
        hidden_add = head_row(2 * q_len, h_len, hidden_width)

        in_one = (normed_one * gains_all[0] + biases_all[0]).astype(BF16)
        projected = dot(in_one, in_full, ((1,), (0,)))
        query_rows = (projected[:, :local_width] + query_add).astype(BF16)
        key_rows = projected[:, local_width : 2 * local_width].astype(BF16)
        value_rows = (projected[:, 2 * local_width :] + value_add).astype(BF16)
        query_rows, grad_all = tie(query_rows, grad_all)
        mixed_rows = attend(query_rows, key_rows, value_rows, segments, score_scale)
        attn_rows = pair.total(dot(mixed_rows, out_t, ((1,), (1,))))
        resid_rows = tok_rows + attn_rows + biases_all[1]
        normed_two, inverse_two = normalize(resid_rows)
        in_two = (normed_two * gains_all[1] + biases_all[2]).astype(BF16)
        pre_act = dot(in_two, up_full, ((1,), (0,))) + hidden_add
        act, slope = gelu_parts(pre_act)
        act_rows = act.astype(BF16)

        g_pre = dot(grad_all, down_t, ((1,), (0,))) * slope
        g_hidden_add = jnp.sum(g_pre, axis=0)
        g_pre_b = g_pre.astype(BF16)
        g_hidden = paired_products([grad_all, in_two], [act_rows, g_pre_b])
        g_pre_b, act_rows, g_hidden = tie(g_pre_b, act_rows, g_hidden)
        g_two_part = dot(g_pre_b, up_full, ((1,), (1,)))
        g_norm_two = pair.total(g_two_part)
        g_hidden_own = lax.psum_scatter(g_hidden, "fsdp", scatter_dimension=0, tiled=True)
        g_down_t, g_up = g_hidden_own[:, :hidden_width], g_hidden_own[:, hidden_width:]
        mlp_part = dot(act_rows, down_t, ((1,), (1,)))
        g_norm_two, mlp_part = tie(g_norm_two, mlp_part.astype(BF16))
        mlp_rows = pair.collect(mlp_part)
        result = (pair.own(resid_rows) + mlp_rows + biases_all[3]).astype(BF16)

        grad_rows = grad_all.astype(F32)
        g_resid = grad_rows + normalize_back(g_norm_two, normed_two, inverse_two, gains_all[1])
        g_resid_b = g_resid.astype(BF16)
        g_mixed = dot(g_resid_b, out_t, ((1,), (0,))).astype(BF16)
        g_query, g_keys, g_values, g_query_add, g_value_add = attend_back(
            query_rows, key_rows, value_rows, g_mixed, segments, score_scale
        )
        g_query_add = jnp.sum(g_query_add, axis=0)
        g_value_add = jnp.sum(g_value_add, axis=0)
        g_proj = jnp.concatenate([g_query, g_keys, g_values], axis=1)
        g_one_part = dot(g_proj, in_full, ((1,), (1,)))

        six_terms = jnp.stack(
            [
                jnp.sum(g_one_part * normed_one, axis=0),
                jnp.sum(g_two_part * normed_two, axis=0),
                jnp.sum(g_one_part, axis=0),
                jnp.sum(pair.own(g_resid), axis=0),
                jnp.sum(g_two_part, axis=0),
                jnp.sum(pair.own(grad_rows), axis=0),
            ]
        )
        six_terms = pair.sum(six_terms)

        def head_blocks(row, length):
            return (
                row.reshape(heads, n_fsdp, length // heads)
                .transpose(1, 0, 2)
                .reshape(n_fsdp, length)
            )

        head_terms = jnp.concatenate(
            [
                head_blocks(g_query_add, q_len),
                head_blocks(g_value_add, q_len),
                head_blocks(g_hidden_add, h_len),
            ],
            axis=1,
        )
        head_terms = jnp.pad(head_terms, ((0, 0), (0, head_count * m - head_terms.shape[1])))
        head_terms = head_terms.reshape(n_fsdp, head_count, m).transpose(1, 0, 2)
        head_terms = head_terms.reshape(head_count, model_width)
        small = jnp.concatenate([six_terms, head_terms], axis=0).astype(BF16)
        spots = jnp.asarray(np.arange(6 + head_count)[:, None] == lanes, BF16)
        small = dot(small, spots, ((0,), (0,))).astype(BF16)

        outer = Scatter(
            ring,
            table,
            [
                dot(in_one, g_proj, ((0,), (0,))).astype(BF16),
                dot(g_resid_b, mixed_rows, ((0,), (0,))).astype(BF16),
                small,
            ],
        )
        outer.step()
        g_one_part = outer.before(g_one_part.astype(BF16))
        g_norm_one = pair.collect(g_one_part)
        outer.step()
        tokens_grad = (
            pair.own(g_resid)
            + normalize_back(g_norm_one, pair.own(normed_one), pair.own(inverse_one), gains_all[0])
        ).astype(BF16)
        g_in, g_out_t, small = outer.totals()
        small = small.T
        six_sum = lax.dynamic_slice_in_dim(
            small[:6], lax.axis_index("tensor") * (m // n_tensor), m // n_tensor, 1
        )
        head_sum = small[6 : 6 + head_count].reshape(head_count * m)
        return (
            result,
            tokens_grad,
            g_in.reshape(m, 3, local_width),
            g_out_t.T,
            g_up.astype(F32),
            g_down_t.T.astype(F32),
            head_sum[:q_len].reshape(query_bias.shape),
            head_sum[q_len : 2 * q_len].reshape(value_bias.shape),
            head_sum[2 * q_len : 2 * q_len + h_len].reshape(hidden_bias.shape),
            six_sum[:2],
            six_sum[2:],
        )

    return shards


def solution(mesh):
    n_fsdp = mesh.shape["fsdp"]
    n_tensor = mesh.shape["tensor"]
    rows = P(("fsdp", "tensor"), None)
    columns = P(None, ("fsdp", "tensor"))
    head = P("tensor", "fsdp")
    into = P("fsdp", None, "tensor")
    up = P("fsdp", "tensor")
    return jax.shard_map(
        layer(n_fsdp, n_tensor),
        mesh=mesh,
        in_specs=(
            rows,
            P("fsdp", None),
            columns,
            columns,
            into,
            head,
            head,
            head,
            up,
            head,
            head,
            rows,
        ),
        out_specs=(rows, rows, into, head, up, head, head, head, head, columns, columns),
        check_vma=False,
    )
```

```python
import math

import jax
import jax.numpy as jnp
import numpy as np
from jax import lax
from jax.experimental import pallas as pl
from jax.experimental.pallas import tpu as pltpu
from jax.sharding import PartitionSpec as P

HD = 64
EPS = 1e-05
GELU_C = math.sqrt(2.0 / math.pi)
GELU_A = 0.044715
MASKED = -1e30
BF16 = jnp.bfloat16
F32 = jnp.float32
LANES = 128
VMEM_LIMIT = 48 * 1024 * 1024


def gelu_parts(pre_act):
    square = pre_act * pre_act
    tanh_part = jnp.tanh(GELU_C * pre_act * (1.0 + GELU_A * square))
    half = 0.5 * (1.0 + tanh_part)
    slope = half + 0.5 * pre_act * (1.0 - tanh_part * tanh_part) * GELU_C * (
        1.0 + 3.0 * GELU_A * square
    )
    return pre_act * half, slope


def normalize(row_data):
    row_mean = jnp.mean(row_data, axis=-1, keepdims=True)
    centered = row_data - row_mean
    variance = jnp.mean(centered * centered, axis=-1, keepdims=True)
    inverse = lax.rsqrt(variance + EPS)
    return centered * inverse, inverse


def normalize_back(grad_rows, normed, inverse, gain_row):
    scaled = grad_rows * gain_row
    return inverse * (
        scaled
        - jnp.mean(scaled, axis=-1, keepdims=True)
        - normed * jnp.mean(scaled * normed, axis=-1, keepdims=True)
    )


def tie(*values):
    return lax.optimization_barrier(values)


def assemble(table, pieces, m):
    n = pieces[0].shape[1]
    count = len(pieces)
    total = sum(piece.shape[0] for piece in pieces)

    def copy(places, *refs):
        j = 0
        for i in range(count):
            for own in range(pieces[i].shape[0] // m):
                rows = pl.ds(pl.multiple_of(places[j] * m, m), m)
                refs[count][rows, :] = refs[i][own * m : (own + 1) * m, :]
                j += 1

    return pl.pallas_call(
        copy,
        in_specs=[pl.BlockSpec(memory_space=pltpu.SMEM)]
        + [pl.BlockSpec(memory_space=pltpu.VMEM)] * count,
        out_shape=jax.ShapeDtypeStruct((total, n), pieces[0].dtype),
        compiler_params=pltpu.CompilerParams(vmem_limit_bytes=VMEM_LIMIT),
        name="assemble",
    )(table, *pieces)


def row_blocks(table, sums, at, m, given=None):
    count = len(sums)
    widths = [own.shape[1] for own in sums]

    def read(places, *refs):
        for j, entry in enumerate(at):
            rows = pl.ds(pl.multiple_of(places[entry] * m, m), m)
            start = 0
            for i in range(count):
                spot = (slice(j * m, (j + 1) * m), slice(start, start + widths[i]))
                value = refs[i][rows, :]
                if given is not None:
                    value = (value.astype(F32) + refs[count][spot].astype(F32)).astype(BF16)
                refs[-1][spot] = value
                start += widths[i]

    arrays = [*sums] if given is None else [*sums, given]
    return pl.pallas_call(
        read,
        in_specs=[pl.BlockSpec(memory_space=pltpu.SMEM)]
        + [pl.BlockSpec(memory_space=pltpu.VMEM)] * len(arrays),
        out_shape=jax.ShapeDtypeStruct((len(at) * m, sum(widths)), BF16),
        compiler_params=pltpu.CompilerParams(vmem_limit_bytes=VMEM_LIMIT),
        name="row_blocks",
    )(table, *arrays)


def paired_products(table, lefts, rights, m):
    depth, rows = lefts[0].shape
    width = rights[0].shape[1]
    tile = min(width, 512)
    half = width // tile

    def multiply(places, left_a, left_b, right_a, right_b, own, away, raw, turned):
        j = pl.program_id(0)

        def turn(left):
            raw[...] = left[...].T
            for i in range(rows // m):
                block = pl.ds(pl.multiple_of(places[i] * m, m), m)
                turned[i * m : (i + 1) * m, :] = raw[block, :]

        def product(right):
            own[...] = dot(turned[: rows // 2], right[...], ((1,), (0,))).astype(BF16)
            away[...] = dot(turned[rows // 2 :], right[...], ((1,), (0,))).astype(BF16)

        pl.when(j == 0)(lambda: turn(left_a))
        pl.when(j == half)(lambda: turn(left_b))
        pl.when(j < half)(lambda: product(right_a))
        pl.when(j >= half)(lambda: product(right_b))

    whole = pl.BlockSpec((depth, rows), lambda j: (0, 0))
    return pl.pallas_call(
        multiply,
        grid=(2 * half,),
        in_specs=[
            pl.BlockSpec(memory_space=pltpu.SMEM),
            whole,
            whole,
            pl.BlockSpec((depth, tile), lambda j: (0, jnp.minimum(j, half - 1))),
            pl.BlockSpec((depth, tile), lambda j: (0, jnp.maximum(j - half, 0))),
        ],
        out_specs=[pl.BlockSpec((rows // 2, tile), lambda j: (0, j))] * 2,
        out_shape=[jax.ShapeDtypeStruct((rows // 2, 2 * width), BF16)] * 2,
        scratch_shapes=[pltpu.VMEM((rows, depth), BF16)] * 2,
        compiler_params=pltpu.CompilerParams(vmem_limit_bytes=VMEM_LIMIT),
        name="paired_products",
    )(table, *lefts, *rights)


def allowed_pairs(column, row):
    shape = (column.shape[0], row.shape[1])
    causal = lax.broadcasted_iota(jnp.int32, shape, 0) <= lax.broadcasted_iota(jnp.int32, shape, 1)
    return causal & (column == row)


def probabilities(query, key, allowed):
    scores = jnp.where(allowed, dot(key, query, ((1,), (1,))), MASKED)
    terms = jnp.exp(scores - jnp.max(scores, axis=0, keepdims=True))
    return terms * (1.0 / jnp.sum(terms, axis=0, keepdims=True))


def attend(query_rows, key_rows, value_rows, segments, score_scale):
    seq_count, seq_len = segments.shape
    width = query_rows.shape[1]
    step = min(width, 2 * HD)

    def forward(column, row, query, key, value, mixed):
        allowed = allowed_pairs(column[...], row[0])
        for h in range(step // HD):
            at = slice(h * HD, (h + 1) * HD)
            probs = probabilities(query[:, at] * BF16(score_scale), key[:, at], allowed)
            mixed[:, at] = dot(value[:, at], probs.astype(BF16), ((0,), (0,))).T.astype(BF16)

    rows = pl.BlockSpec((seq_len, step), lambda i, j: (i, j))
    return pl.pallas_call(
        forward,
        grid=(seq_count, width // step),
        in_specs=[
            pl.BlockSpec((seq_len, 1), lambda i, j: (i, 0)),
            pl.BlockSpec((1, 1, seq_len), lambda i, j: (i, 0, 0)),
            rows,
            rows,
            rows,
        ],
        out_specs=rows,
        out_shape=jax.ShapeDtypeStruct(query_rows.shape, BF16),
        compiler_params=pltpu.CompilerParams(vmem_limit_bytes=VMEM_LIMIT),
        name="attend",
    )(
        segments.reshape(-1, 1),
        segments.reshape(seq_count, 1, seq_len),
        query_rows,
        key_rows,
        value_rows,
    )


def attend_back(query_rows, key_rows, value_rows, g_mixed, segments, score_scale):
    seq_count, seq_len = segments.shape
    width = query_rows.shape[1]
    step = min(width, 2 * HD)

    def backward(column, row, query, key, value, grad, g_query, g_key, g_value, sum_q, sum_v):
        allowed = allowed_pairs(column[...], row[0])
        for h in range(step // HD):
            at = slice(h * HD, (h + 1) * HD)
            q, k, v, g = query[:, at] * BF16(score_scale), key[:, at], value[:, at], grad[:, at]
            probs = probabilities(q, k, allowed)
            g_probs = dot(v, g, ((1,), (1,)))
            inner = jnp.sum(probs * g_probs, axis=0, keepdims=True)
            g_scores = (probs * (g_probs - inner)).astype(BF16)
            gv = dot(probs.astype(BF16), g, ((1,), (0,)))
            gq = dot(k, g_scores, ((0,), (0,))).T * score_scale
            g_query[:, at] = gq.astype(BF16)
            g_key[:, at] = dot(g_scores, q, ((1,), (0,))).astype(BF16)
            g_value[:, at] = gv.astype(BF16)
            sum_q[0, :, at] = jnp.sum(gq, axis=0, keepdims=True)
            sum_v[0, :, at] = jnp.sum(gv, axis=0, keepdims=True)

    rows = pl.BlockSpec((seq_len, step), lambda i, j: (i, j))
    sums = pl.BlockSpec((1, 1, step), lambda i, j: (i, 0, j))
    wide = jax.ShapeDtypeStruct(query_rows.shape, BF16)
    total = jax.ShapeDtypeStruct((seq_count, 1, width), F32)
    return pl.pallas_call(
        backward,
        grid=(seq_count, width // step),
        in_specs=[
            pl.BlockSpec((seq_len, 1), lambda i, j: (i, 0)),
            pl.BlockSpec((1, 1, seq_len), lambda i, j: (i, 0, 0)),
            rows,
            rows,
            rows,
            rows,
        ],
        out_specs=[rows, rows, rows, sums, sums],
        out_shape=[wide, wide, wide, total, total],
        compiler_params=pltpu.CompilerParams(vmem_limit_bytes=VMEM_LIMIT),
        name="attend_back",
    )(
        segments.reshape(-1, 1),
        segments.reshape(seq_count, 1, seq_len),
        query_rows,
        key_rows,
        value_rows,
        g_mixed,
    )


def dot(left, right, dims):
    return lax.dot_general(left, right, (dims, ((), ())), preferred_element_type=F32)


def pieces_of(value):
    pieces = []
    for _ in range(3):
        piece = lax.reduce_precision(value, 8, 7)
        pieces.append(piece.astype(BF16))
        value = value - piece
    return pieces


class Ring:
    def __init__(self, n_fsdp):
        self.size = n_fsdp
        self.chips = n_fsdp // 2
        second = n_fsdp // 8
        first = self.chips // second
        cycle = [(a, 0) for a in range(first)]
        for a in reversed(range(first)):
            across = list(range(1, second))
            cycle += [(a, b) for b in (across if a % 2 else reversed(across))]
        self.cycle = [a * second + b for a, b in cycle]
        self.place = {chip: p for p, chip in enumerate(self.cycle)}
        rows = []
        for device in range(n_fsdp):
            chip, core = device // 2, device % 2
            back = [self.cycle[(self.place[chip] - k) % self.chips] for k in range(self.chips)]
            rows.append([2 * c + core for c in back] + [2 * c + 1 - core for c in back])
        self.tables = np.asarray(rows, np.int32)
        along = [[2 * chip + core for chip in self.cycle] for core in range(2)]
        self.groups = along
        self.places = np.asarray([along[0] + along[1], along[1] + along[0]], np.int32)

    def table(self):
        return jnp.asarray(self.tables)[lax.axis_index("fsdp")]

    def along(self):
        return jnp.asarray(self.places)[lax.axis_index("fsdp") % 2]

    def gather(self, block):
        return lax.all_gather(block, "fsdp", axis=0, tiled=True, axis_index_groups=self.groups)

    def scatter(self, own):
        return lax.psum_scatter(
            own, "fsdp", scatter_dimension=0, tiled=True, axis_index_groups=self.groups
        )

    def hop(self, value, core=0, along=0):
        pairs = []
        for source in range(self.size):
            place = (self.place[source // 2] + along) % self.chips
            pairs.append((source, 2 * self.cycle[place] + (source + core) % 2))
        return lax.ppermute(value, "fsdp", pairs)


class Gather:
    def __init__(self, ring, block):
        self.ring = ring
        self.up, self.down = [block], [block]

    def step(self):
        if len(self.up) <= self.ring.chips // 2:
            self.up.append(self.ring.hop(self.up[-1], along=1))
        if len(self.down) <= (self.ring.chips - 1) // 2:
            self.down.append(self.ring.hop(self.down[-1], along=-1))

    def before(self, *values):
        values = tie(*values, self.up[-1], self.down[-1])[: len(values)]
        return values if len(values) > 1 else values[0]

    def whole(self, table):
        while len(self.up) <= self.ring.chips // 2:
            self.step()
        own = self.up + self.down[:0:-1]
        m = own[0].shape[0]
        return assemble(table, own + [self.ring.hop(piece, core=1) for piece in own], m)


class Pair:
    def __init__(self, n_tensor):
        self.size = n_tensor

    def swap(self, value):
        return lax.ppermute(value, "tensor", [(0, 1), (1, 0)])

    def spread(self, own):
        if self.size != 2:
            return lax.all_gather(own, "tensor", axis=0, tiled=True)
        other = self.swap(own)
        first = lax.axis_index("tensor") == 0
        return jnp.concatenate(
            [jnp.where(first, own, other), jnp.where(first, other, own)], axis=0
        )

    def total(self, partial_rows):
        rounded = partial_rows.astype(BF16)
        if self.size != 2:
            return lax.psum(rounded.astype(F32), "tensor")
        return rounded.astype(F32) + self.swap(rounded).astype(F32)

    def collect(self, partial_rows, after=None):
        rounded = partial_rows.astype(BF16)
        if self.size != 2:
            return lax.psum_scatter(rounded, "tensor", scatter_dimension=0, tiled=True).astype(F32)
        rows = rounded.shape[0] // 2
        index = lax.axis_index("tensor")
        away = lax.dynamic_slice_in_dim(rounded, (1 - index) * rows, rows, 0)
        stay = lax.dynamic_slice_in_dim(rounded, index * rows, rows, 0)
        other = self.swap(away)
        if after is not None:
            other, _ = tie(other, after)
        return stay.astype(F32) + other.astype(F32)

    def sum(self, terms):
        if self.size != 2:
            return lax.psum(terms, "tensor")
        return terms + self.swap(terms)

    def own(self, rows_all):
        rows = rows_all.shape[0] // self.size
        return lax.dynamic_slice_in_dim(rows_all, lax.axis_index("tensor") * rows, rows, 0)


def layer(n_fsdp, n_tensor):
    ring = Ring(n_fsdp)
    pair = Pair(n_tensor)

    def shards(
        tokens,
        segments,
        norm_gains,
        row_biases,
        attention_in,
        query_bias,
        value_bias,
        attention_out,
        hidden_in,
        hidden_bias,
        hidden_out,
        output_grad,
    ):
        m = attention_in.shape[0]
        model_width = m * n_fsdp
        local_width = attention_in.shape[2]
        heads = query_bias.shape[0]
        hidden_width = hidden_in.shape[1]
        score_scale = 1.0 / math.sqrt(HD)
        q_len, h_len = query_bias.size, hidden_bias.size

        table = ring.table()
        along = ring.along()
        six = pair.spread(jnp.concatenate([norm_gains, row_biases], axis=0).T)
        head_flat = jnp.concatenate(
            [query_bias.reshape(q_len), value_bias.reshape(q_len), hidden_bias.reshape(h_len)]
        )
        head_count = -(-head_flat.size // m)
        head_flat = jnp.pad(head_flat, (0, head_count * m - head_flat.size))
        columns = jnp.concatenate(
            pieces_of(six) + [head_flat.reshape(head_count, m).T],
            axis=1,
        )
        columns = jnp.pad(columns, ((0, 0), (0, LANES - columns.shape[1])))
        one = Gather(
            ring,
            jnp.concatenate(
                [attention_in.reshape(m, 3 * local_width), attention_out.T, columns], axis=1
            ),
        )
        one.step()
        hidden_block = jnp.concatenate([hidden_in, hidden_out.T], axis=1)
        one.step()
        hidden_half = ring.gather(one.before(hidden_block))
        tok_rows = pair.spread(one.before(tokens)).astype(F32)
        one.step()
        grad_all = pair.spread(one.before(output_grad))
        normed_one, inverse_one = normalize(tok_rows)
        one_full = one.whole(table)
        in_full = one_full[:, : 3 * local_width]
        out_t = one_full[:, 3 * local_width : 4 * local_width]
        columns = one_full[:, 4 * local_width :]
        lanes = np.arange(LANES)[None, :]
        is_six = (lanes < 18) & (lanes % 6 == np.arange(6)[:, None])
        is_head = lanes == 18 + np.arange(head_count)[:, None]
        picked = np.concatenate([is_six, is_head], axis=0)
        picked = dot(jnp.asarray(picked, BF16), columns, ((1,), (1,)))
        gains_all, biases_all = picked[:2], picked[2:6]
        head_small = picked[6:].reshape(head_count, n_fsdp, m).transpose(1, 0, 2)
        head_small = head_small.reshape(n_fsdp, head_count * m)

        def head_row(start, length, width):
            return (
                head_small[:, start : start + length]
                .reshape(n_fsdp, heads, length // heads)
                .transpose(1, 0, 2)
                .reshape(width)
            )

        query_add = head_row(0, q_len, local_width)
        value_add = head_row(q_len, q_len, local_width)
        hidden_add = head_row(2 * q_len, h_len, hidden_width)

        in_one = (normed_one * gains_all[0] + biases_all[0]).astype(BF16)
        projected = dot(in_one, in_full, ((1,), (0,)))
        query_rows = (projected[:, :local_width] + query_add).astype(BF16)
        key_rows = projected[:, local_width : 2 * local_width].astype(BF16)
        value_rows = (projected[:, 2 * local_width :] + value_add).astype(BF16)
        query_rows, grad_all = tie(query_rows, grad_all)
        mixed_rows = attend(query_rows, key_rows, value_rows, segments, score_scale)
        attn_part = dot(mixed_rows, out_t, ((1,), (1,))).astype(BF16)
        hidden_half, _ = tie(hidden_half, attn_part)
        attn_rows = pair.total(attn_part)
        hidden_full = assemble(along, [hidden_half, ring.hop(hidden_half, core=1)], m)
        up_full, down_t = hidden_full[:, :hidden_width], hidden_full[:, hidden_width:]
        resid_rows = tok_rows + attn_rows + biases_all[1]
        normed_two, inverse_two = normalize(resid_rows)
        in_two = (normed_two * gains_all[1] + biases_all[2]).astype(BF16)
        pre_act = dot(in_two, up_full, ((1,), (0,))) + hidden_add
        act, slope = gelu_parts(pre_act)
        act_rows = act.astype(BF16)

        g_pre = dot(grad_all, down_t, ((1,), (0,))) * slope
        g_hidden_add = jnp.sum(g_pre, axis=0)
        g_pre_b = g_pre.astype(BF16)
        hidden_own, hidden_away = paired_products(
            along, [grad_all, in_two], [act_rows, g_pre_b], m
        )
        g_pre_b, act_rows, hidden_away = tie(g_pre_b, act_rows, hidden_away)
        g_two_part = dot(g_pre_b, up_full, ((1,), (1,)))
        g_norm_two = pair.total(g_two_part)
        hidden_own = hidden_own.astype(F32) + ring.hop(hidden_away, core=1).astype(F32)
        hidden_own = hidden_own.astype(BF16)
        g_hidden_own = ring.scatter(hidden_own)
        mlp_part = dot(act_rows, down_t, ((1,), (1,)))
        mlp_part = mlp_part.astype(BF16)
        g_norm_two, _, _ = tie(g_norm_two, mlp_part, hidden_own)

        grad_rows = grad_all.astype(F32)
        g_resid = grad_rows + normalize_back(g_norm_two, normed_two, inverse_two, gains_all[1])
        g_resid_b = g_resid.astype(BF16)
        g_mixed = dot(g_resid_b, out_t, ((1,), (0,))).astype(BF16)
        mlp_rows = pair.collect(mlp_part, g_mixed)
        result = (pair.own(resid_rows) + mlp_rows + biases_all[3]).astype(BF16)
        g_query, g_keys, g_values, g_query_add, g_value_add = attend_back(
            query_rows, key_rows, value_rows, g_mixed, segments, score_scale
        )
        g_query_add = jnp.sum(g_query_add, axis=0)
        g_value_add = jnp.sum(g_value_add, axis=0)
        g_query, result = tie(g_query, result)
        g_proj = jnp.concatenate([g_query, g_keys, g_values], axis=1)
        g_one_part = dot(g_proj, in_full, ((1,), (1,)))

        six_terms = jnp.stack(
            [
                jnp.sum(g_one_part * normed_one, axis=0),
                jnp.sum(g_two_part * normed_two, axis=0),
                jnp.sum(g_one_part, axis=0),
                jnp.sum(pair.own(g_resid), axis=0),
                jnp.sum(g_two_part, axis=0),
                jnp.sum(pair.own(grad_rows), axis=0),
            ]
        )
        six_terms = pair.sum(six_terms)

        def head_blocks(row, length):
            return (
                row.reshape(heads, n_fsdp, length // heads)
                .transpose(1, 0, 2)
                .reshape(n_fsdp, length)
            )

        head_terms = jnp.concatenate(
            [
                head_blocks(g_query_add, q_len),
                head_blocks(g_value_add, q_len),
                head_blocks(g_hidden_add, h_len),
            ],
            axis=1,
        )
        head_terms = jnp.pad(head_terms, ((0, 0), (0, head_count * m - head_terms.shape[1])))
        head_terms = head_terms.reshape(n_fsdp, head_count, m).transpose(1, 0, 2)
        head_terms = head_terms.reshape(head_count, model_width)
        small = jnp.concatenate([six_terms, head_terms], axis=0).astype(BF16)
        spots = jnp.asarray(np.arange(6 + head_count)[:, None] == lanes, BF16)
        small = dot(small, spots, ((0,), (0,))).astype(BF16)

        sums = [
            dot(in_one, g_proj, ((0,), (0,))).astype(BF16),
            dot(g_resid_b, mixed_rows, ((0,), (0,))).astype(BF16),
            small,
        ]
        away = row_blocks(along, sums, range(ring.chips, 2 * ring.chips), m)
        arrived = ring.hop(away, core=1)
        outer_own = row_blocks(along, sums, range(ring.chips), m, arrived)
        g_one_part, _ = tie(g_one_part.astype(BF16), outer_own)
        outer_own, g_hidden_own = tie(outer_own, g_hidden_own)
        outer_own = ring.scatter(outer_own)
        g_norm_one = pair.collect(g_one_part)
        tokens_grad = (
            pair.own(g_resid)
            + normalize_back(g_norm_one, pair.own(normed_one), pair.own(inverse_one), gains_all[0])
        ).astype(BF16)
        g_down_t, g_up = g_hidden_own[:, :hidden_width], g_hidden_own[:, hidden_width:]
        outer_own = outer_own.astype(F32)
        g_in = outer_own[:, : 3 * local_width]
        g_out_t = outer_own[:, 3 * local_width : 4 * local_width]
        small = outer_own[:, 4 * local_width :].T
        six_sum = lax.dynamic_slice_in_dim(
            small[:6], lax.axis_index("tensor") * (m // n_tensor), m // n_tensor, 1
        )
        head_sum = small[6 : 6 + head_count].reshape(head_count * m)
        return (
            result,
            tokens_grad,
            g_in.reshape(m, 3, local_width),
            g_out_t.T,
            g_up.astype(F32),
            g_down_t.T.astype(F32),
            head_sum[:q_len].reshape(query_bias.shape),
            head_sum[q_len : 2 * q_len].reshape(value_bias.shape),
            head_sum[2 * q_len : 2 * q_len + h_len].reshape(hidden_bias.shape),
            six_sum[:2],
            six_sum[2:],
        )

    return shards


def solution(mesh):
    n_fsdp = mesh.shape["fsdp"]
    n_tensor = mesh.shape["tensor"]
    rows = P(("fsdp", "tensor"), None)
    columns = P(None, ("fsdp", "tensor"))
    head = P("tensor", "fsdp")
    into = P("fsdp", None, "tensor")
    up = P("fsdp", "tensor")
    return jax.shard_map(
        layer(n_fsdp, n_tensor),
        mesh=mesh,
        in_specs=(
            rows,
            P("fsdp", None),
            columns,
            columns,
            into,
            head,
            head,
            head,
            up,
            head,
            head,
            rows,
        ),
        out_specs=(rows, rows, into, head, up, head, head, head, head, columns, columns),
        check_vma=False,
    )
```

```python
import math

import jax
import jax.numpy as jnp
import numpy as np
from jax import lax
from jax.experimental import pallas as pl
from jax.experimental.pallas import tpu as pltpu
from jax.sharding import PartitionSpec as P

HD = 64
EPS = 1e-05
GELU_C = math.sqrt(2.0 / math.pi)
GELU_A = 0.044715
MASKED = -1e30
BF16 = jnp.bfloat16
F32 = jnp.float32
LANES = 128
VMEM_LIMIT = 48 * 1024 * 1024


def gelu_parts(pre_act):
    square = pre_act * pre_act
    tanh_part = jnp.tanh(GELU_C * pre_act * (1.0 + GELU_A * square))
    half = 0.5 * (1.0 + tanh_part)
    slope = half + 0.5 * pre_act * (1.0 - tanh_part * tanh_part) * GELU_C * (
        1.0 + 3.0 * GELU_A * square
    )
    return pre_act * half, slope


def normalize(row_data):
    row_mean = jnp.mean(row_data, axis=-1, keepdims=True)
    centered = row_data - row_mean
    variance = jnp.mean(centered * centered, axis=-1, keepdims=True)
    inverse = lax.rsqrt(variance + EPS)
    return centered * inverse, inverse


def normalize_back(grad_rows, normed, inverse, gain_row):
    scaled = grad_rows * gain_row
    return inverse * (
        scaled
        - jnp.mean(scaled, axis=-1, keepdims=True)
        - normed * jnp.mean(scaled * normed, axis=-1, keepdims=True)
    )


def tie(*values):
    return lax.optimization_barrier(values)


def assemble(table, pieces, m):
    n = pieces[0].shape[1]
    count = len(pieces)
    total = sum(piece.shape[0] for piece in pieces)

    def copy(places, *refs):
        j = 0
        for i in range(count):
            for own in range(pieces[i].shape[0] // m):
                rows = pl.ds(pl.multiple_of(places[j] * m, m), m)
                refs[count][rows, :] = refs[i][own * m : (own + 1) * m, :]
                j += 1

    return pl.pallas_call(
        copy,
        in_specs=[pl.BlockSpec(memory_space=pltpu.SMEM)]
        + [pl.BlockSpec(memory_space=pltpu.VMEM)] * count,
        out_shape=jax.ShapeDtypeStruct((total, n), pieces[0].dtype),
        compiler_params=pltpu.CompilerParams(vmem_limit_bytes=VMEM_LIMIT),
        name="assemble",
    )(table, *pieces)


def row_blocks(table, sums, at, m, given=None):
    count = len(sums)
    widths = [own.shape[1] for own in sums]

    def read(places, *refs):
        for j, entry in enumerate(at):
            rows = pl.ds(pl.multiple_of(places[entry] * m, m), m)
            start = 0
            for i in range(count):
                spot = (slice(j * m, (j + 1) * m), slice(start, start + widths[i]))
                value = refs[i][rows, :]
                if given is not None:
                    value = (value.astype(F32) + refs[count][spot].astype(F32)).astype(BF16)
                refs[-1][spot] = value
                start += widths[i]

    arrays = [*sums] if given is None else [*sums, given]
    return pl.pallas_call(
        read,
        in_specs=[pl.BlockSpec(memory_space=pltpu.SMEM)]
        + [pl.BlockSpec(memory_space=pltpu.VMEM)] * len(arrays),
        out_shape=jax.ShapeDtypeStruct((len(at) * m, sum(widths)), BF16),
        compiler_params=pltpu.CompilerParams(vmem_limit_bytes=VMEM_LIMIT),
        name="row_blocks",
    )(table, *arrays)


def paired_products(table, lefts, rights, m):
    depth, rows = lefts[0].shape
    width = rights[0].shape[1]
    tile = min(width, 512)
    half = width // tile

    def multiply(places, left_a, left_b, right_a, right_b, own, away, raw, turned):
        j = pl.program_id(0)

        def turn(left):
            raw[...] = left[...].T
            for i in range(rows // m):
                block = pl.ds(pl.multiple_of(places[i] * m, m), m)
                turned[i * m : (i + 1) * m, :] = raw[block, :]

        def product(right):
            own[...] = dot(turned[: rows // 2], right[...], ((1,), (0,))).astype(BF16)
            away[...] = dot(turned[rows // 2 :], right[...], ((1,), (0,))).astype(BF16)

        pl.when(j == 0)(lambda: turn(left_a))
        pl.when(j == half)(lambda: turn(left_b))
        pl.when(j < half)(lambda: product(right_a))
        pl.when(j >= half)(lambda: product(right_b))

    whole = pl.BlockSpec((depth, rows), lambda j: (0, 0))
    return pl.pallas_call(
        multiply,
        grid=(2 * half,),
        in_specs=[
            pl.BlockSpec(memory_space=pltpu.SMEM),
            whole,
            whole,
            pl.BlockSpec((depth, tile), lambda j: (0, jnp.minimum(j, half - 1))),
            pl.BlockSpec((depth, tile), lambda j: (0, jnp.maximum(j - half, 0))),
        ],
        out_specs=[pl.BlockSpec((rows // 2, tile), lambda j: (0, j))] * 2,
        out_shape=[jax.ShapeDtypeStruct((rows // 2, 2 * width), BF16)] * 2,
        scratch_shapes=[pltpu.VMEM((rows, depth), BF16)] * 2,
        compiler_params=pltpu.CompilerParams(vmem_limit_bytes=VMEM_LIMIT),
        name="paired_products",
    )(table, *lefts, *rights)


def allowed_pairs(column, row):
    shape = (column.shape[0], row.shape[1])
    causal = lax.broadcasted_iota(jnp.int32, shape, 0) <= lax.broadcasted_iota(jnp.int32, shape, 1)
    return causal & (column == row)


def probabilities(query, key, allowed):
    scores = jnp.where(allowed, dot(key, query, ((1,), (1,))), MASKED)
    terms = jnp.exp(scores - jnp.max(scores, axis=0, keepdims=True))
    return terms * (1.0 / jnp.sum(terms, axis=0, keepdims=True))


def attend(query_rows, key_rows, value_rows, segments, score_scale):
    seq_count, seq_len = segments.shape
    width = query_rows.shape[1]
    step = min(width, 2 * HD)

    def forward(column, row, query, key, value, mixed):
        allowed = allowed_pairs(column[...], row[0])
        for h in range(step // HD):
            at = slice(h * HD, (h + 1) * HD)
            probs = probabilities(query[:, at] * BF16(score_scale), key[:, at], allowed)
            mixed[:, at] = dot(value[:, at], probs.astype(BF16), ((0,), (0,))).T.astype(BF16)

    rows = pl.BlockSpec((seq_len, step), lambda i, j: (i, j))
    return pl.pallas_call(
        forward,
        grid=(seq_count, width // step),
        in_specs=[
            pl.BlockSpec((seq_len, 1), lambda i, j: (i, 0)),
            pl.BlockSpec((1, 1, seq_len), lambda i, j: (i, 0, 0)),
            rows,
            rows,
            rows,
        ],
        out_specs=rows,
        out_shape=jax.ShapeDtypeStruct(query_rows.shape, BF16),
        compiler_params=pltpu.CompilerParams(vmem_limit_bytes=VMEM_LIMIT),
        name="attend",
    )(
        segments.reshape(-1, 1),
        segments.reshape(seq_count, 1, seq_len),
        query_rows,
        key_rows,
        value_rows,
    )


def attend_back(query_rows, key_rows, value_rows, g_mixed, segments, score_scale):
    seq_count, seq_len = segments.shape
    width = query_rows.shape[1]
    step = min(width, 2 * HD)

    def backward(column, row, query, key, value, grad, g_query, g_key, g_value, sum_q, sum_v):
        allowed = allowed_pairs(column[...], row[0])
        for h in range(step // HD):
            at = slice(h * HD, (h + 1) * HD)
            q, k, v, g = query[:, at] * BF16(score_scale), key[:, at], value[:, at], grad[:, at]
            probs = probabilities(q, k, allowed)
            g_probs = dot(v, g, ((1,), (1,)))
            inner = jnp.sum(probs * g_probs, axis=0, keepdims=True)
            g_scores = (probs * (g_probs - inner)).astype(BF16)
            gv = dot(probs.astype(BF16), g, ((1,), (0,)))
            gq = dot(k, g_scores, ((0,), (0,))).T * score_scale
            g_query[:, at] = gq.astype(BF16)
            g_key[:, at] = dot(g_scores, q, ((1,), (0,))).astype(BF16)
            g_value[:, at] = gv.astype(BF16)
            sum_q[0, :, at] = jnp.sum(gq, axis=0, keepdims=True)
            sum_v[0, :, at] = jnp.sum(gv, axis=0, keepdims=True)

    rows = pl.BlockSpec((seq_len, step), lambda i, j: (i, j))
    sums = pl.BlockSpec((1, 1, step), lambda i, j: (i, 0, j))
    wide = jax.ShapeDtypeStruct(query_rows.shape, BF16)
    total = jax.ShapeDtypeStruct((seq_count, 1, width), F32)
    return pl.pallas_call(
        backward,
        grid=(seq_count, width // step),
        in_specs=[
            pl.BlockSpec((seq_len, 1), lambda i, j: (i, 0)),
            pl.BlockSpec((1, 1, seq_len), lambda i, j: (i, 0, 0)),
            rows,
            rows,
            rows,
            rows,
        ],
        out_specs=[rows, rows, rows, sums, sums],
        out_shape=[wide, wide, wide, total, total],
        compiler_params=pltpu.CompilerParams(vmem_limit_bytes=VMEM_LIMIT),
        name="attend_back",
    )(
        segments.reshape(-1, 1),
        segments.reshape(seq_count, 1, seq_len),
        query_rows,
        key_rows,
        value_rows,
        g_mixed,
    )


def dot(left, right, dims):
    return lax.dot_general(left, right, (dims, ((), ())), preferred_element_type=F32)


def pieces_of(value):
    pieces = []
    for _ in range(3):
        piece = lax.reduce_precision(value, 8, 7)
        pieces.append(piece.astype(BF16))
        value = value - piece
    return pieces


class Ring:
    def __init__(self, n_fsdp):
        self.size = n_fsdp
        self.chips = n_fsdp // 2
        second = n_fsdp // 8
        first = self.chips // second
        cycle = [(a, 0) for a in range(first)]
        for a in reversed(range(first)):
            across = list(range(1, second))
            cycle += [(a, b) for b in (across if a % 2 else reversed(across))]
        self.cycle = [a * second + b for a, b in cycle]
        self.place = {chip: p for p, chip in enumerate(self.cycle)}
        rows = []
        for device in range(n_fsdp):
            chip, core = device // 2, device % 2
            back = [self.cycle[(self.place[chip] - k) % self.chips] for k in range(self.chips)]
            rows.append([2 * c + core for c in back] + [2 * c + 1 - core for c in back])
        self.tables = np.asarray(rows, np.int32)
        along = [[2 * chip + core for chip in self.cycle] for core in range(2)]
        self.groups = along
        self.places = np.asarray([along[0] + along[1], along[1] + along[0]], np.int32)

    def table(self):
        return jnp.asarray(self.tables)[lax.axis_index("fsdp")]

    def along(self):
        return jnp.asarray(self.places)[lax.axis_index("fsdp") % 2]

    def gather(self, block):
        return lax.all_gather(block, "fsdp", axis=0, tiled=True, axis_index_groups=self.groups)

    def scatter(self, own):
        return lax.psum_scatter(
            own, "fsdp", scatter_dimension=0, tiled=True, axis_index_groups=self.groups
        )

    def hop(self, value, core=0, along=0):
        pairs = []
        for source in range(self.size):
            place = (self.place[source // 2] + along) % self.chips
            pairs.append((source, 2 * self.cycle[place] + (source + core) % 2))
        return lax.ppermute(value, "fsdp", pairs)


class Gather:
    def __init__(self, ring, block):
        self.ring = ring
        self.up, self.down = [block], [block]

    def step(self):
        if len(self.up) <= self.ring.chips // 2:
            self.up.append(self.ring.hop(self.up[-1], along=1))
        if len(self.down) <= (self.ring.chips - 1) // 2:
            self.down.append(self.ring.hop(self.down[-1], along=-1))

    def before(self, *values):
        values = tie(*values, self.up[-1], self.down[-1])[: len(values)]
        return values if len(values) > 1 else values[0]

    def whole(self, table):
        while len(self.up) <= self.ring.chips // 2:
            self.step()
        own = self.up + self.down[:0:-1]
        m = own[0].shape[0]
        return assemble(table, own + [self.ring.hop(piece, core=1) for piece in own], m)


class Pair:
    def __init__(self, n_tensor):
        self.size = n_tensor

    def swap(self, value):
        return lax.ppermute(value, "tensor", [(0, 1), (1, 0)])

    def spread(self, own):
        if self.size != 2:
            return lax.all_gather(own, "tensor", axis=0, tiled=True)
        other = self.swap(own)
        first = lax.axis_index("tensor") == 0
        return jnp.concatenate(
            [jnp.where(first, own, other), jnp.where(first, other, own)], axis=0
        )

    def total(self, partial_rows):
        rounded = partial_rows.astype(BF16)
        if self.size != 2:
            return lax.psum(rounded.astype(F32), "tensor")
        return rounded.astype(F32) + self.swap(rounded).astype(F32)

    def collect(self, partial_rows, after=None):
        rounded = partial_rows.astype(BF16)
        if self.size != 2:
            return lax.psum_scatter(rounded, "tensor", scatter_dimension=0, tiled=True).astype(F32)
        rows = rounded.shape[0] // 2
        index = lax.axis_index("tensor")
        away = lax.dynamic_slice_in_dim(rounded, (1 - index) * rows, rows, 0)
        stay = lax.dynamic_slice_in_dim(rounded, index * rows, rows, 0)
        other = self.swap(away)
        if after is not None:
            other, _ = tie(other, after)
        return stay.astype(F32) + other.astype(F32)

    def sum(self, terms):
        if self.size != 2:
            return lax.psum(terms, "tensor")
        return terms + self.swap(terms)

    def own(self, rows_all):
        rows = rows_all.shape[0] // self.size
        return lax.dynamic_slice_in_dim(rows_all, lax.axis_index("tensor") * rows, rows, 0)


def layer(n_fsdp, n_tensor):
    ring = Ring(n_fsdp)
    pair = Pair(n_tensor)

    def shards(
        tokens,
        segments,
        norm_gains,
        row_biases,
        attention_in,
        query_bias,
        value_bias,
        attention_out,
        hidden_in,
        hidden_bias,
        hidden_out,
        output_grad,
    ):
        m = attention_in.shape[0]
        model_width = m * n_fsdp
        local_width = attention_in.shape[2]
        heads = query_bias.shape[0]
        hidden_width = hidden_in.shape[1]
        score_scale = 1.0 / math.sqrt(HD)
        q_len, h_len = query_bias.size, hidden_bias.size

        table = ring.table()
        along = ring.along()
        six = pair.spread(jnp.concatenate([norm_gains, row_biases], axis=0).T)
        head_flat = jnp.concatenate(
            [query_bias.reshape(q_len), value_bias.reshape(q_len), hidden_bias.reshape(h_len)]
        )
        head_count = -(-head_flat.size // m)
        head_flat = jnp.pad(head_flat, (0, head_count * m - head_flat.size))
        columns = jnp.concatenate(
            pieces_of(six) + [head_flat.reshape(head_count, m).T],
            axis=1,
        )
        columns = jnp.pad(columns, ((0, 0), (0, LANES - columns.shape[1])))
        one = Gather(
            ring,
            jnp.concatenate(
                [attention_in.reshape(m, 3 * local_width), attention_out.T, columns], axis=1
            ),
        )
        one.step()
        hidden_block = jnp.concatenate([hidden_in, hidden_out.T], axis=1)
        one.step()
        hidden_half = ring.gather(one.before(hidden_block))
        tok_rows = pair.spread(one.before(tokens)).astype(F32)
        one.step()
        grad_all = pair.spread(one.before(output_grad))
        normed_one, inverse_one = normalize(tok_rows)
        one_full = one.whole(table)
        in_full = one_full[:, : 3 * local_width]
        out_t = one_full[:, 3 * local_width : 4 * local_width]
        columns = one_full[:, 4 * local_width :]
        lanes = np.arange(LANES)[None, :]
        is_six = (lanes < 18) & (lanes % 6 == np.arange(6)[:, None])
        is_head = lanes == 18 + np.arange(head_count)[:, None]
        picked = np.concatenate([is_six, is_head], axis=0)
        picked = dot(jnp.asarray(picked, BF16), columns, ((1,), (1,)))
        gains_all, biases_all = picked[:2], picked[2:6]
        head_small = picked[6:].reshape(head_count, n_fsdp, m).transpose(1, 0, 2)
        head_small = head_small.reshape(n_fsdp, head_count * m)

        def head_row(start, length, width):
            return (
                head_small[:, start : start + length]
                .reshape(n_fsdp, heads, length // heads)
                .transpose(1, 0, 2)
                .reshape(width)
            )

        query_add = head_row(0, q_len, local_width)
        value_add = head_row(q_len, q_len, local_width)
        hidden_add = head_row(2 * q_len, h_len, hidden_width)

        in_one = (normed_one * gains_all[0] + biases_all[0]).astype(BF16)
        projected = dot(in_one, in_full, ((1,), (0,)))
        query_rows = (projected[:, :local_width] + query_add).astype(BF16)
        key_rows = projected[:, local_width : 2 * local_width].astype(BF16)
        value_rows = (projected[:, 2 * local_width :] + value_add).astype(BF16)
        query_rows, grad_all = tie(query_rows, grad_all)
        mixed_rows = attend(query_rows, key_rows, value_rows, segments, score_scale)
        attn_part = dot(mixed_rows, out_t, ((1,), (1,))).astype(BF16)
        hidden_half, _ = tie(hidden_half, attn_part)
        attn_rows = pair.total(attn_part)
        hidden_full = assemble(along, [hidden_half, ring.hop(hidden_half, core=1)], m)
        up_full, down_t = hidden_full[:, :hidden_width], hidden_full[:, hidden_width:]
        resid_rows = tok_rows + attn_rows + biases_all[1]
        normed_two, inverse_two = normalize(resid_rows)
        in_two = (normed_two * gains_all[1] + biases_all[2]).astype(BF16)
        pre_act = dot(in_two, up_full, ((1,), (0,))) + hidden_add
        act, slope = gelu_parts(pre_act)
        act_rows = act.astype(BF16)

        g_pre = dot(grad_all, down_t, ((1,), (0,))) * slope
        g_hidden_add = jnp.sum(g_pre, axis=0)
        g_pre_b = g_pre.astype(BF16)
        g_two_part = dot(g_pre_b, up_full, ((1,), (1,)))
        g_two_rounded = g_two_part.astype(BF16)
        g_norm_two = pair.total(g_two_rounded)
        g_pre_b, act_rows, _ = tie(g_pre_b, act_rows, g_two_rounded)
        hidden_own, hidden_away = paired_products(
            along, [grad_all, in_two], [act_rows, g_pre_b], m
        )
        hidden_own = hidden_own.astype(F32) + ring.hop(hidden_away, core=1).astype(F32)
        hidden_own = hidden_own.astype(BF16)
        mlp_part = dot(act_rows, down_t, ((1,), (1,)))
        mlp_part = mlp_part.astype(BF16)
        g_norm_two, mlp_part, hidden_own = tie(g_norm_two, mlp_part, hidden_own)
        g_hidden_own = ring.scatter(hidden_own)

        grad_rows = grad_all.astype(F32)
        g_resid = grad_rows + normalize_back(g_norm_two, normed_two, inverse_two, gains_all[1])
        g_resid_b = g_resid.astype(BF16)
        g_mixed = dot(g_resid_b, out_t, ((1,), (0,))).astype(BF16)
        mlp_rows = pair.collect(mlp_part, g_mixed)
        result = (pair.own(resid_rows) + mlp_rows + biases_all[3]).astype(BF16)
        g_query, g_keys, g_values, g_query_add, g_value_add = attend_back(
            query_rows, key_rows, value_rows, g_mixed, segments, score_scale
        )
        g_query_add = jnp.sum(g_query_add, axis=0)
        g_value_add = jnp.sum(g_value_add, axis=0)
        g_query, result = tie(g_query, result)
        g_proj = jnp.concatenate([g_query, g_keys, g_values], axis=1)
        g_one_part = dot(g_proj, in_full, ((1,), (1,)))

        six_terms = jnp.stack(
            [
                jnp.sum(g_one_part * normed_one, axis=0),
                jnp.sum(g_two_part * normed_two, axis=0),
                jnp.sum(g_one_part, axis=0),
                jnp.sum(pair.own(g_resid), axis=0),
                jnp.sum(g_two_part, axis=0),
                jnp.sum(pair.own(grad_rows), axis=0),
            ]
        )
        six_terms = pair.sum(six_terms)

        def head_blocks(row, length):
            return (
                row.reshape(heads, n_fsdp, length // heads)
                .transpose(1, 0, 2)
                .reshape(n_fsdp, length)
            )

        head_terms = jnp.concatenate(
            [
                head_blocks(g_query_add, q_len),
                head_blocks(g_value_add, q_len),
                head_blocks(g_hidden_add, h_len),
            ],
            axis=1,
        )
        head_terms = jnp.pad(head_terms, ((0, 0), (0, head_count * m - head_terms.shape[1])))
        head_terms = head_terms.reshape(n_fsdp, head_count, m).transpose(1, 0, 2)
        head_terms = head_terms.reshape(head_count, model_width)
        small = jnp.concatenate([six_terms, head_terms], axis=0).astype(BF16)
        spots = jnp.asarray(np.arange(6 + head_count)[:, None] == lanes, BF16)
        small = dot(small, spots, ((0,), (0,))).astype(BF16)

        sums = [
            dot(in_one, g_proj, ((0,), (0,))).astype(BF16),
            dot(g_resid_b, mixed_rows, ((0,), (0,))).astype(BF16),
            small,
        ]
        away = row_blocks(along, sums, range(ring.chips, 2 * ring.chips), m)
        arrived = ring.hop(away, core=1)
        outer_own = row_blocks(along, sums, range(ring.chips), m, arrived)
        g_one_part, _ = tie(g_one_part.astype(BF16), outer_own)
        outer_own, g_hidden_own = tie(outer_own, g_hidden_own)
        outer_own = ring.scatter(outer_own)
        g_norm_one = pair.collect(g_one_part)
        tokens_grad = (
            pair.own(g_resid)
            + normalize_back(g_norm_one, pair.own(normed_one), pair.own(inverse_one), gains_all[0])
        ).astype(BF16)
        g_down_t, g_up = g_hidden_own[:, :hidden_width], g_hidden_own[:, hidden_width:]
        outer_own = outer_own.astype(F32)
        g_in = outer_own[:, : 3 * local_width]
        g_out_t = outer_own[:, 3 * local_width : 4 * local_width]
        small = outer_own[:, 4 * local_width :].T
        six_sum = lax.dynamic_slice_in_dim(
            small[:6], lax.axis_index("tensor") * (m // n_tensor), m // n_tensor, 1
        )
        head_sum = small[6 : 6 + head_count].reshape(head_count * m)
        return (
            result,
            tokens_grad,
            g_in.reshape(m, 3, local_width),
            g_out_t.T,
            g_up.astype(F32),
            g_down_t.T.astype(F32),
            head_sum[:q_len].reshape(query_bias.shape),
            head_sum[q_len : 2 * q_len].reshape(value_bias.shape),
            head_sum[2 * q_len : 2 * q_len + h_len].reshape(hidden_bias.shape),
            six_sum[:2],
            six_sum[2:],
        )

    return shards


def solution(mesh):
    n_fsdp = mesh.shape["fsdp"]
    n_tensor = mesh.shape["tensor"]
    rows = P(("fsdp", "tensor"), None)
    columns = P(None, ("fsdp", "tensor"))
    head = P("tensor", "fsdp")
    into = P("fsdp", None, "tensor")
    up = P("fsdp", "tensor")
    return jax.shard_map(
        layer(n_fsdp, n_tensor),
        mesh=mesh,
        in_specs=(
            rows,
            P("fsdp", None),
            columns,
            columns,
            into,
            head,
            head,
            head,
            up,
            head,
            head,
            rows,
        ),
        out_specs=(rows, rows, into, head, up, head, head, head, head, columns, columns),
        check_vma=False,
    )
```
